256 devices in a mesh: dp: 8 (over x, core), section: 4 (over y), seq: 8 (over z).
Axes of the slice: x: 4, y: 4, z: 8, core: 2. Of those that a mesh axis runs over, the one named last changes fastest.
Arguments:
- clips_in: bfloat16 [16, 8, 128, 1280], P('dp', None, 'seq'), may hold values from -6 to 6
- w_qkv: bfloat16 [4, 1280, 1920], P('section'), may hold values from -1 to 1
- w_out: bfloat16 [4, 640, 1280], P('section'), may hold values from -0.25 to 0.25
- out_cotangent: bfloat16 [16, 8, 128, 1280], P('dp', 'seq'), may hold values from -0.046875 to 0.046875
Outputs:
- section_outputs: bfloat16 [4, 16, 8, 128, 1280], P('section', 'dp', 'seq')
- grad_qkv: float32 [4, 1280, 1920], P('section', ('dp', 'seq'))
- grad_out_t: float32 [4, 1280, 640], P('section', ('dp', 'seq'))
The draws below stay inside these ranges and needn't reach their ends.
All inputs are finite; a program needn't handle non-finite values.
Results may differ from the reference program's by a relative error of at most 0.025.
Values may be sent and summed in bfloat16 or wider, within the bound.
A program may use at most 128 MiB of HBM per device.

```python
import math
import jax
import jax.numpy as jnp
from jax import lax

D = 1280
HEADS = 10
HD = 640
SECTIONS = 4
FRAMES = 8
PATCHES = 128
CLIPS = 16


def draw_w_qkv(key, part):
    shape_all = (SECTIONS, D, 3 * HD)
    limit_value = 4.5 / math.sqrt(D)
    base_draw = jax.random.normal(jax.random.fold_in(key, 11), shape_all, jnp.float32) / math.sqrt(D)
    base_draw = jnp.clip(base_draw, -limit_value, limit_value)
    return base_draw.astype(jnp.bfloat16)


def block_scale(stream_key, dims, cuts, smallest, high):
    gain, own = 1.0, jax.random.fold_in(stream_key, 6)
    for position, blocks in cuts:
        heights = jnp.exp(jax.random.uniform(jax.random.fold_in(own, position), (blocks,), jnp.float32, smallest / len(cuts), high / len(cuts)))
        gain = gain * jnp.repeat(heights, dims[position] // blocks).reshape([-1 if axis == position else 1 for axis in range(len(dims))])
    return gain


def normal_values(stream_key, shape, deviation, bound, shards=(), held_as=jnp.bfloat16):
    drawn = deviation * jax.random.normal(stream_key, shape, jnp.float32)
    if shards:
        drawn = drawn * block_scale(stream_key, shape, shards, -0.22, 0.18)
    return jnp.clip(drawn, -bound, bound).astype(held_as)


def setup_inputs(seed: int = 0) -> dict:
    keys = jax.random.split(jax.random.key(seed), 5)
    return {
        "clips_in": normal_values(keys[0], (CLIPS, FRAMES, PATCHES, D), 1.0, 6.0, ((0, 8), (2, 8))),
        "w_qkv": draw_w_qkv(jax.random.fold_in(keys[4], 71), 0),
        "w_out": normal_values(keys[2], (SECTIONS, HD, D), HD ** -0.5, 0.25, ((0, 4),)),
        "out_cotangent": normal_values(keys[3], (CLIPS, FRAMES, PATCHES, D), ((CLIPS * FRAMES * PATCHES) ** -0.5), 0.046875, ((0, 8), (1, 8))),
    }


norm_eps = 1e-05

def normalize(token_rows):
    values = token_rows.astype(jnp.float32)
    centred = values - lax.optimization_barrier(jnp.mean(values, axis=-1, keepdims=True))
    inverse = lax.rsqrt(lax.optimization_barrier(jnp.mean(centred * centred, axis=-1, keepdims=True)) + norm_eps)
    return (centred * inverse, inverse)

def split_heads(packed, groups, heads):
    row_count, all_cols = packed.shape
    head_block = all_cols // 3
    length = row_count // groups
    head_dim = head_block // heads
    pieces = [packed[:, piece_idx * head_block:(piece_idx + 1) * head_block].reshape(groups, length, heads, head_dim) for piece_idx in range(3)]
    return (pieces[0], pieces[1], pieces[2])

def softmax_rows(query_heads, key_heads, score_scale):
    scores = jnp.einsum('glhe,gmhe->ghlm', query_heads.astype(jnp.float32), key_heads.astype(jnp.float32)) * score_scale
    row_max = lax.optimization_barrier(jnp.max(scores, axis=-1, keepdims=True))
    exp_scores = jnp.exp(scores - row_max)
    return exp_scores / lax.optimization_barrier(jnp.sum(exp_scores, axis=-1, keepdims=True))

def project(token_rows, weight_qkv, groups, heads):
    unit_rows, _ = normalize(token_rows)
    normed = unit_rows.astype(jnp.bfloat16)
    packed = jnp.dot(normed, weight_qkv, preferred_element_type=jnp.float32).astype(jnp.bfloat16)
    query_heads, key_heads, value_heads = split_heads(packed, groups, heads)
    score_scale = 1.0 / math.sqrt(query_heads.shape[-1])
    probs_low = softmax_rows(query_heads, key_heads, score_scale).astype(jnp.bfloat16)
    mixed_heads = jnp.einsum('ghlm,gmhe->glhe', probs_low.astype(jnp.float32), value_heads.astype(jnp.float32))
    return (packed, mixed_heads.astype(jnp.bfloat16).reshape(token_rows.shape[0], -1))

def backward_rows(token_rows, packed, mixed_heads, weight_qkv, weight_out, grad_rows, groups, heads):
    unit_rows, inverse = normalize(token_rows)
    normed = unit_rows.astype(jnp.bfloat16)
    d_mixed = jnp.dot(grad_rows, weight_out.T, preferred_element_type=jnp.float32).astype(jnp.bfloat16)
    grad_out_term = jnp.dot(grad_rows.T, mixed_heads, preferred_element_type=jnp.float32)
    query_heads, key_heads, value_heads = split_heads(packed, groups, heads)
    score_scale = 1.0 / math.sqrt(query_heads.shape[-1])
    probs = softmax_rows(query_heads, key_heads, score_scale)
    probs_low = probs.astype(jnp.bfloat16)
    d_heads = d_mixed.reshape(query_heads.shape).astype(jnp.float32)
    d_values = jnp.einsum('ghlm,glhe->gmhe', probs_low.astype(jnp.float32), d_heads)
    d_probs = jnp.einsum('glhe,gmhe->ghlm', d_heads, value_heads.astype(jnp.float32))
    d_scores = (probs * (d_probs - lax.optimization_barrier(jnp.sum(probs * d_probs, axis=-1, keepdims=True)))).astype(jnp.bfloat16)
    d_query = jnp.einsum('ghlm,gmhe->glhe', d_scores.astype(jnp.float32), key_heads.astype(jnp.float32)) * score_scale
    d_keys = jnp.einsum('ghlm,glhe->gmhe', d_scores.astype(jnp.float32), query_heads.astype(jnp.float32)) * score_scale
    row_count = token_rows.shape[0]
    d_packed = jnp.concatenate([d_query.reshape(row_count, -1), d_keys.reshape(row_count, -1), d_values.reshape(row_count, -1)], axis=-1).astype(jnp.bfloat16)
    grad_qkv_term = jnp.dot(normed.T, d_packed, preferred_element_type=jnp.float32)
    d_normed = jnp.dot(d_packed, weight_qkv.T, preferred_element_type=jnp.float32)
    d_inside = inverse * (d_normed - lax.optimization_barrier(jnp.mean(d_normed, axis=-1, keepdims=True)) - unit_rows * lax.optimization_barrier(jnp.mean(d_normed * unit_rows, axis=-1, keepdims=True)))
    back_rows = (grad_rows.astype(jnp.float32) + d_inside).astype(jnp.bfloat16)
    return (back_rows, grad_qkv_term, grad_out_term)

def to_rows(clip_now, parity):
    if parity == 0:
        return (clip_now.transpose(1, 0, 2).reshape(-1, clip_now.shape[2]), clip_now.shape[1])
    return (clip_now.reshape(-1, clip_now.shape[2]), clip_now.shape[0])

def from_rows(token_rows, clip_shape, parity):
    if parity == 0:
        return token_rows.reshape(clip_shape[1], clip_shape[0], clip_shape[2]).transpose(1, 0, 2)
    return token_rows.reshape(clip_shape)

def reference(clips_in, w_qkv, w_out, out_cotangent):
    section_total = w_qkv.shape[0]

    def one_clip(totals, inputs_pair):
        clip_now, seed_grad = inputs_pair
        saved_parts = []
        outputs = []
        for section_index in range(section_total):
            parity = section_index % 2
            token_rows, groups = to_rows(clip_now, parity)
            packed, mixed_heads = project(token_rows, w_qkv[section_index], groups, HEADS)
            result = (token_rows.astype(jnp.float32) + jnp.dot(mixed_heads, w_out[section_index], preferred_element_type=jnp.float32)).astype(jnp.bfloat16)
            saved_parts.append((token_rows, packed, mixed_heads, groups))
            clip_now = from_rows(result, clip_now.shape, parity)
            outputs.append(clip_now)
        grad_clip = seed_grad
        terms_qkv = [None] * section_total
        terms_out = [None] * section_total
        for section_index in reversed(range(section_total)):
            parity = section_index % 2
            token_rows, packed, mixed_heads, groups = saved_parts[section_index]
            grad_rows, _ = to_rows(grad_clip, parity)
            back_rows, grad_qkv_term, grad_out_term = backward_rows(token_rows, packed, mixed_heads, w_qkv[section_index], w_out[section_index], grad_rows, groups, HEADS)
            terms_qkv[section_index] = grad_qkv_term
            terms_out[section_index] = grad_out_term
            grad_clip = from_rows(back_rows, grad_clip.shape, parity)
        totals = (totals[0] + jnp.stack(terms_qkv), totals[1] + jnp.stack(terms_out))
        return (totals, jnp.stack(outputs))
    start_totals = (jnp.zeros(w_qkv.shape, jnp.float32), jnp.zeros((w_out.shape[0], w_out.shape[2], w_out.shape[1]), jnp.float32))
    totals, outputs = lax.scan(one_clip, start_totals, (clips_in, out_cotangent))
    return (outputs.transpose(1, 0, 2, 3, 4), totals[0], totals[1])
```

```python
import functools
import math

import jax
import jax.numpy as jnp
from jax import lax
from jax.experimental import pallas as pl
from jax.experimental.pallas import tpu as pltpu
from jax.sharding import PartitionSpec as P

HEAD_DIM = 64
NORM_EPS = 1e-05
MASKED = -1e30
MESH = pl.DeviceIdType.MESH


def dot(a, b, a_dim, b_dim):
    return lax.dot_general(
        a, b, (((a_dim,), (b_dim,)), ((), ())), preferred_element_type=jnp.float32
    )


def relay_kernel(
    seq_count,
    section_count,
    x_hbm,
    w_qkv_hbm,
    w_out_hbm,
    g_hbm,
    out_hbm,
    grad_qkv_ref,
    grad_out_ref,
    wq,
    wo,
    xb,
    gb,
    ub,
    rb,
    nb,
    pk,
    pr,
    mx,
    dpk,
    hb,
    bb,
    in_sem,
    x_send,
    x_recv,
    g_send,
    g_recv,
    o_send,
    o_recv,
):
    dp_id = lax.axis_index("dp")
    section = lax.axis_index("section")
    seq_id = lax.axis_index("seq")
    micro_count, rows, width = xb.shape
    block = rows // seq_count
    inner = wo.shape[0]
    pairs = inner // (2 * HEAD_DIM)
    scale = 1.0 / math.sqrt(HEAD_DIM)
    is_first = section == 0
    is_last = section == section_count - 1
    is_odd = lax.rem(section, 2) == 1

    load_wq = pltpu.make_async_copy(w_qkv_hbm, wq, in_sem.at[0])
    load_wo = pltpu.make_async_copy(w_out_hbm, wo, in_sem.at[1])
    load_x = pltpu.make_async_copy(x_hbm, xb, in_sem.at[2])
    load_g = pltpu.make_async_copy(g_hbm, gb, in_sem.at[3])

    @pl.when(is_first)
    def _():
        load_x.start()

    load_wq.start()
    load_wo.start()

    @pl.when(is_last)
    def _():
        load_g.start()

    barrier = pltpu.get_barrier_semaphore()

    @pl.when(section > 0)
    def _():
        for k in range(seq_count):
            pl.semaphore_signal(
                barrier, inc=1, device_id=(dp_id, section - 1, k), device_id_type=MESH
            )

    @pl.when(section < section_count - 1)
    def _():
        for k in range(seq_count):
            pl.semaphore_signal(
                barrier, inc=1, device_id=(dp_id, section + 1, k), device_id_type=MESH
            )

    inner_section = jnp.logical_and(section > 0, section < section_count - 1)
    pl.semaphore_wait(barrier, jnp.where(inner_section, 2 * seq_count, seq_count))

    def hop(src, dst, send, recv, m, k, step):
        return pltpu.make_async_remote_copy(
            src_ref=src.at[m, pl.ds(k * block, block), :],
            dst_ref=dst.at[m, pl.ds(seq_id * block, block), :],
            send_sem=send.at[m, k],
            recv_sem=recv.at[m, seq_id],
            device_id=(dp_id, section + step, k),
            device_id_type=MESH,
        )

    def arrival(dst, recv, m, k):
        landed = dst.at[m, pl.ds(k * block, block), :]
        return pltpu.make_async_copy(landed, landed, recv.at[m, k])

    def output_back(m):
        return pltpu.make_async_remote_copy(
            src_ref=xb.at[m],
            dst_ref=out_hbm.at[m],
            send_sem=o_send.at[m],
            recv_sem=o_recv.at[m],
            device_id=(dp_id, section - 1, seq_id),
            device_id_type=MESH,
        )

    def output_own(m):
        return pltpu.make_async_copy(hb.at[m], out_hbm.at[m], o_recv.at[m])

    lane = lax.broadcasted_iota(jnp.int32, (rows, 2 * HEAD_DIM), 1)
    first_head = lane < HEAD_DIM
    row_group = lax.rem(lax.broadcasted_iota(jnp.int32, (2 * rows, rows), 0), block)
    col_group = lax.rem(lax.broadcasted_iota(jnp.int32, (2 * rows, rows), 1), block)
    same_group = jnp.where(row_group == col_group, 1, 0) + jnp.where(is_odd, 1, 0) > 0

    def stacked(part):
        zero = jnp.zeros_like(part)
        return jnp.concatenate(
            [jnp.where(first_head, part, zero), jnp.where(first_head, zero, part)], axis=0
        )

    def joined(part):
        return jnp.where(first_head, part[:rows], part[rows:])

    def forward(m, carry):
        @pl.when(section > 0)
        def _():
            for k in range(seq_count):
                arrival(xb, x_recv, m, k).wait()

        @pl.when(is_odd)
        def _():
            output_back(m).start()

        values = xb[m].astype(jnp.float32)
        centred = values - jnp.mean(values, axis=-1, keepdims=True)
        inverse = lax.rsqrt(jnp.mean(centred * centred, axis=-1, keepdims=True) + NORM_EPS)
        unit = centred * inverse
        ub[m] = unit
        rb[m] = jnp.broadcast_to(inverse, (rows, 128))
        nb[m] = unit.astype(jnp.bfloat16)
        pk[m] = dot(nb[m], wq[...], 1, 0).astype(jnp.bfloat16)
        for p in range(pairs):
            cols = pl.ds(p * 128, 128)
            query = pk[m, :, pl.ds(p * 128, 128)]
            key = pk[m, :, pl.ds(inner + p * 128, 128)]
            value = pk[m, :, pl.ds(2 * inner + p * 128, 128)]
            scores = dot(stacked(query), key, 1, 1) * scale
            scores = jnp.where(same_group, scores, MASKED)
            exps = jnp.exp(scores - jnp.max(scores, axis=-1, keepdims=True))
            probs = exps / jnp.sum(exps, axis=-1, keepdims=True)
            pr[m, p] = probs
            mx[m, :, cols] = joined(dot(probs.astype(jnp.bfloat16), value, 1, 0)).astype(
                jnp.bfloat16
            )
        hb[m] = (xb[m].astype(jnp.float32) + dot(mx[m], wo[...], 1, 0)).astype(jnp.bfloat16)

        @pl.when(section < section_count - 1)
        def _():
            for k in range(seq_count):
                hop(hb, xb, x_send, x_recv, m, k, 1).start()

        @pl.when(is_odd)
        def _():
            output_own(m).start()

        return carry

    def backward(m, carry):
        @pl.when(section < section_count - 1)
        def _():
            for k in range(seq_count):
                arrival(gb, g_recv, m, k).wait()

        d_mixed = dot(gb[m], wo[...], 1, 1).astype(jnp.bfloat16)
        for p in range(pairs):
            query = stacked(pk[m, :, pl.ds(p * 128, 128)])
            key = pk[m, :, pl.ds(inner + p * 128, 128)]
            value = pk[m, :, pl.ds(2 * inner + p * 128, 128)]
            d_heads = stacked(d_mixed[:, p * 128 : (p + 1) * 128])
            probs = pr[m, p]
            d_values = dot(probs.astype(jnp.bfloat16), d_heads, 0, 0)
            d_probs = dot(d_heads, value, 1, 1)
            d_scores = probs * (d_probs - jnp.sum(probs * d_probs, axis=-1, keepdims=True))
            d_scores = d_scores.astype(jnp.bfloat16)
            d_query = joined(dot(d_scores, key, 1, 0)) * scale
            d_keys = dot(d_scores, query, 0, 0) * scale
            dpk[m, :, pl.ds(p * 128, 128)] = d_query.astype(jnp.bfloat16)
            dpk[m, :, pl.ds(inner + p * 128, 128)] = d_keys.astype(jnp.bfloat16)
            dpk[m, :, pl.ds(2 * inner + p * 128, 128)] = d_values.astype(jnp.bfloat16)

        @pl.when(section > 0)
        def _():
            d_normed = dot(dpk[m], wq[...], 1, 1)
            unit = ub[m]
            d_inside = rb[m, :, 0:1] * (
                d_normed
                - jnp.mean(d_normed, axis=-1, keepdims=True)
                - unit * jnp.mean(d_normed * unit, axis=-1, keepdims=True)
            )
            bb[m] = (gb[m].astype(jnp.float32) + d_inside).astype(jnp.bfloat16)
            for k in range(seq_count):
                hop(bb, gb, g_send, g_recv, m, k, -1).start()

        return carry

    @pl.when(is_first)
    def _():
        load_x.wait()

    load_wq.wait()
    load_wo.wait()
    lax.fori_loop(0, micro_count, forward, 0)

    @pl.when(is_last)
    def _():
        load_g.wait()

    lax.fori_loop(0, micro_count, backward, 0)

    chunk = 256 if width % 256 == 0 else 128

    def weight_grads(i, carry):
        cols = pl.ds(pl.multiple_of(i * chunk, chunk), chunk)
        normed = nb[:, :, cols].reshape(micro_count * rows, chunk)
        grads = gb[:, :, cols].reshape(micro_count * rows, chunk)
        d_packed = dpk[...].reshape(micro_count * rows, 3 * inner)
        mixed = mx[...].reshape(micro_count * rows, inner)
        grad_qkv_ref[cols, :] = dot(normed, d_packed, 0, 0).astype(jnp.bfloat16)
        grad_out_ref[cols, :] = dot(grads, mixed, 0, 0).astype(jnp.bfloat16)
        return carry

    lax.fori_loop(0, width // chunk, weight_grads, 0)

    for m in range(micro_count):

        @pl.when(section < section_count - 1)
        def _():
            for k in range(seq_count):
                hop(hb, xb, x_send, x_recv, m, k, 1).wait_send()

        @pl.when(section > 0)
        def _():
            for k in range(seq_count):
                hop(bb, gb, g_send, g_recv, m, k, -1).wait_send()

        @pl.when(is_odd)
        def _():
            output_back(m).wait_send()
            output_own(m).wait()

        @pl.when(jnp.logical_not(is_odd))
        def _():
            pltpu.make_async_copy(out_hbm.at[m], out_hbm.at[m], o_recv.at[m]).wait()


def relay(seq_count, section_count, x, w_qkv, w_out, g):
    micro_count, rows, width = x.shape
    inner = w_out.shape[0]
    pairs = inner // (2 * HEAD_DIM)
    bf16, f32 = jnp.bfloat16, jnp.float32
    tokens = (micro_count, rows, width)
    dma = pltpu.SemaphoreType.DMA
    any_spec = pl.BlockSpec(memory_space=pl.ANY)
    vmem_spec = pl.BlockSpec(memory_space=pltpu.VMEM)
    return pl.pallas_call(
        functools.partial(relay_kernel, seq_count, section_count),
        out_shape=(
            jax.ShapeDtypeStruct(tokens, bf16),
            jax.ShapeDtypeStruct((width, 3 * inner), bf16),
            jax.ShapeDtypeStruct((width, inner), bf16),
        ),
        in_specs=[any_spec] * 4,
        out_specs=(any_spec, vmem_spec, vmem_spec),
        scratch_shapes=[
            pltpu.VMEM((width, 3 * inner), bf16),
            pltpu.VMEM((inner, width), bf16),
            pltpu.VMEM(tokens, bf16),
            pltpu.VMEM(tokens, bf16),
            pltpu.VMEM(tokens, f32),
            pltpu.VMEM((micro_count, rows, 128), f32),
            pltpu.VMEM(tokens, bf16),
            pltpu.VMEM((micro_count, rows, 3 * inner), bf16),
            pltpu.VMEM((micro_count, pairs, 2 * rows, rows), f32),
            pltpu.VMEM((micro_count, rows, inner), bf16),
            pltpu.VMEM((micro_count, rows, 3 * inner), bf16),
            pltpu.VMEM(tokens, bf16),
            pltpu.VMEM(tokens, bf16),
            dma((4,)),
            dma((micro_count, seq_count)),
            dma((micro_count, seq_count)),
            dma((micro_count, seq_count)),
            dma((micro_count, seq_count)),
            dma((micro_count,)),
            dma((micro_count,)),
        ],
        compiler_params=pltpu.CompilerParams(
            collective_id=0, has_side_effects=True, vmem_limit_bytes=60 * 1024 * 1024
        ),
        name="relay",
    )(x, w_qkv, w_out, g)


def local(clips_in, w_qkv, w_out, out_cotangent):
    seq_count = lax.axis_size("seq")
    section_count = lax.axis_size("section")
    micro_count, frames, patches_dev, width = clips_in.shape
    x = clips_in.reshape(micro_count, frames * patches_dev, width)
    g = out_cotangent.reshape(micro_count, -1, width)
    outputs, grad_qkv, grad_out = relay(seq_count, section_count, x, w_qkv[0], w_out[0], g)
    shards = []
    for part in (grad_qkv, grad_out):
        group = lax.axis_size("dp") * seq_count
        blocks = part.reshape(group, part.shape[0] // group, part.shape[1])
        shard = lax.psum_scatter(blocks, ("dp", "seq"), scatter_dimension=0, tiled=False)
        shards.append(shard.astype(jnp.float32))
    return (
        outputs.reshape((1,) + out_cotangent.shape),
        shards[0][None],
        shards[1][None],
    )


def solution(mesh):
    return jax.shard_map(
        local,
        mesh=mesh,
        in_specs=(
            P("dp", None, "seq", None),
            P("section", None, None),
            P("section", None, None),
            P("dp", "seq", None, None),
        ),
        out_specs=(
            P("section", "dp", "seq", None, None),
            P("section", ("dp", "seq"), None),
            P("section", ("dp", "seq"), None),
        ),
        check_vma=False,
    )
```

```python
import functools
import math

import jax
import jax.numpy as jnp
from jax import lax
from jax.experimental import pallas as pl
from jax.experimental.pallas import tpu as pltpu
from jax.sharding import PartitionSpec as P

HEAD_DIM = 64
NORM_EPS = 1e-05
MASKED = -1e30
MESH = pl.DeviceIdType.MESH


def dot(a, b, a_dim, b_dim):
    return lax.dot_general(
        a, b, (((a_dim,), (b_dim,)), ((), ())), preferred_element_type=jnp.float32
    )


def relay_kernel(
    seq_count,
    section_count,
    x_hbm,
    w_qkv_hbm,
    w_out_hbm,
    g_hbm,
    out_hbm,
    grad_qkv_ref,
    grad_out_ref,
    wq,
    wo,
    xb,
    gb,
    ub,
    rb,
    nb,
    pk,
    pr,
    mx,
    dpk,
    hb,
    bb,
    in_sem,
    x_send,
    x_recv,
    g_send,
    g_recv,
    o_send,
    o_recv,
    cw,
    core_in,
    xs,
    x_in,
    block_sum,
    zs,
    z_in,
    core_send,
    core_recv,
    ring_x_send,
    ring_x_recv,
    ring_z_send,
    ring_z_recv,
):
    dp_id = lax.axis_index("dp")
    section = lax.axis_index("section")
    seq_id = lax.axis_index("seq")
    micro_count, rows, width = xb.shape
    block = rows // seq_count
    inner = wo.shape[0]
    pairs = inner // (2 * HEAD_DIM)
    scale = 1.0 / math.sqrt(HEAD_DIM)
    dp_count = lax.axis_size("dp")
    x_count = dp_count // 2
    x_id = dp_id // 2
    core = lax.rem(dp_id, 2)
    is_first = section == 0
    is_last = section == section_count - 1
    is_odd = lax.rem(section, 2) == 1

    load_wq = pltpu.make_async_copy(w_qkv_hbm, wq, in_sem.at[0])
    load_wo = pltpu.make_async_copy(w_out_hbm, wo, in_sem.at[1])
    load_x = pltpu.make_async_copy(x_hbm, xb, in_sem.at[2])
    load_g = pltpu.make_async_copy(g_hbm, gb, in_sem.at[3])

    @pl.when(is_first)
    def _():
        load_x.start()

    load_wq.start()
    load_wo.start()

    @pl.when(is_last)
    def _():
        load_g.start()

    barrier = pltpu.get_barrier_semaphore()

    @pl.when(section > 0)
    def _():
        for k in range(seq_count):
            pl.semaphore_signal(
                barrier, inc=1, device_id=(dp_id, section - 1, k), device_id_type=MESH
            )

    @pl.when(section < section_count - 1)
    def _():
        for k in range(seq_count):
            pl.semaphore_signal(
                barrier, inc=1, device_id=(dp_id, section + 1, k), device_id_type=MESH
            )

    def at_x(step):
        return (2 * lax.rem(x_id + step + x_count, x_count) + core, section, seq_id)

    def at_z(step):
        return (dp_id, section, lax.rem(seq_id + step + seq_count, seq_count))

    other_core = (2 * x_id + 1 - core, section, seq_id)
    for peer in (other_core, at_x(1), at_x(-1), at_z(1), at_z(-1)):
        pl.semaphore_signal(barrier, inc=1, device_id=peer, device_id_type=MESH)
    inner_section = jnp.logical_and(section > 0, section < section_count - 1)
    pl.semaphore_wait(barrier, jnp.where(inner_section, 2 * seq_count + 5, seq_count + 5))

    def hop(src, dst, send, recv, m, k, step):
        return pltpu.make_async_remote_copy(
            src_ref=src.at[m, pl.ds(k * block, block), :],
            dst_ref=dst.at[m, pl.ds(seq_id * block, block), :],
            send_sem=send.at[m, k],
            recv_sem=recv.at[m, seq_id],
            device_id=(dp_id, section + step, k),
            device_id_type=MESH,
        )

    def arrival(dst, recv, m, k):
        landed = dst.at[m, pl.ds(k * block, block), :]
        return pltpu.make_async_copy(landed, landed, recv.at[m, k])

    def output_back(m):
        return pltpu.make_async_remote_copy(
            src_ref=xb.at[m],
            dst_ref=out_hbm.at[m],
            send_sem=o_send.at[m],
            recv_sem=o_recv.at[m],
            device_id=(dp_id, section - 1, seq_id),
            device_id_type=MESH,
        )

    def output_own(m):
        return pltpu.make_async_copy(hb.at[m], out_hbm.at[m], o_recv.at[m])

    lane = lax.broadcasted_iota(jnp.int32, (rows, 2 * HEAD_DIM), 1)
    first_head = lane < HEAD_DIM
    row_group = lax.rem(lax.broadcasted_iota(jnp.int32, (2 * rows, rows), 0), block)
    col_group = lax.rem(lax.broadcasted_iota(jnp.int32, (2 * rows, rows), 1), block)
    same_group = jnp.where(row_group == col_group, 1, 0) + jnp.where(is_odd, 1, 0) > 0

    def stacked(part):
        zero = jnp.zeros_like(part)
        return jnp.concatenate(
            [jnp.where(first_head, part, zero), jnp.where(first_head, zero, part)], axis=0
        )

    def joined(part):
        return jnp.where(first_head, part[:rows], part[rows:])

    def forward(m, carry):
        @pl.when(section > 0)
        def _():
            for k in range(seq_count):
                arrival(xb, x_recv, m, k).wait()

        @pl.when(is_odd)
        def _():
            output_back(m).start()

        values = xb[m].astype(jnp.float32)
        centred = values - jnp.mean(values, axis=-1, keepdims=True)
        inverse = lax.rsqrt(jnp.mean(centred * centred, axis=-1, keepdims=True) + NORM_EPS)
        unit = centred * inverse
        ub[m] = unit
        rb[m] = jnp.broadcast_to(inverse, (rows, 128))
        nb[m] = unit.astype(jnp.bfloat16)
        pk[m] = dot(nb[m], wq[...], 1, 0).astype(jnp.bfloat16)
        for p in range(pairs):
            cols = pl.ds(p * 128, 128)
            query = pk[m, :, pl.ds(p * 128, 128)]
            key = pk[m, :, pl.ds(inner + p * 128, 128)]
            value = pk[m, :, pl.ds(2 * inner + p * 128, 128)]
            scores = dot(stacked(query), key, 1, 1) * scale
            scores = jnp.where(same_group, scores, MASKED)
            exps = jnp.exp(scores - jnp.max(scores, axis=-1, keepdims=True))
            probs = exps / jnp.sum(exps, axis=-1, keepdims=True)
            pr[m, p] = probs
            mx[m, :, cols] = joined(dot(probs.astype(jnp.bfloat16), value, 1, 0)).astype(
                jnp.bfloat16
            )
        hb[m] = (xb[m].astype(jnp.float32) + dot(mx[m], wo[...], 1, 0)).astype(jnp.bfloat16)

        @pl.when(section < section_count - 1)
        def _():
            for k in range(seq_count):
                hop(hb, xb, x_send, x_recv, m, k, 1).start()

        @pl.when(is_odd)
        def _():
            output_own(m).start()

        return carry

    def backward(m, carry):
        @pl.when(section < section_count - 1)
        def _():
            for k in range(seq_count):
                arrival(gb, g_recv, m, k).wait()

        d_mixed = dot(gb[m], wo[...], 1, 1).astype(jnp.bfloat16)
        for p in range(pairs):
            query = stacked(pk[m, :, pl.ds(p * 128, 128)])
            key = pk[m, :, pl.ds(inner + p * 128, 128)]
            value = pk[m, :, pl.ds(2 * inner + p * 128, 128)]
            d_heads = stacked(d_mixed[:, p * 128 : (p + 1) * 128])
            probs = pr[m, p]
            d_values = dot(probs.astype(jnp.bfloat16), d_heads, 0, 0)
            d_probs = dot(d_heads, value, 1, 1)
            d_scores = probs * (d_probs - jnp.sum(probs * d_probs, axis=-1, keepdims=True))
            d_scores = d_scores.astype(jnp.bfloat16)
            d_query = joined(dot(d_scores, key, 1, 0)) * scale
            d_keys = dot(d_scores, query, 0, 0) * scale
            dpk[m, :, pl.ds(p * 128, 128)] = d_query.astype(jnp.bfloat16)
            dpk[m, :, pl.ds(inner + p * 128, 128)] = d_keys.astype(jnp.bfloat16)
            dpk[m, :, pl.ds(2 * inner + p * 128, 128)] = d_values.astype(jnp.bfloat16)

        @pl.when(section > 0)
        def _():
            d_normed = dot(dpk[m], wq[...], 1, 1)
            unit = ub[m]
            d_inside = rb[m, :, 0:1] * (
                d_normed
                - jnp.mean(d_normed, axis=-1, keepdims=True)
                - unit * jnp.mean(d_normed * unit, axis=-1, keepdims=True)
            )
            bb[m] = (gb[m].astype(jnp.float32) + d_inside).astype(jnp.bfloat16)
            for k in range(seq_count):
                hop(bb, gb, g_send, g_recv, m, k, -1).start()

        return carry

    @pl.when(is_first)
    def _():
        load_x.wait()

    load_wq.wait()
    load_wo.wait()
    lax.fori_loop(0, micro_count, forward, 0)

    @pl.when(is_last)
    def _():
        load_g.wait()

    lax.fori_loop(0, micro_count, backward, 0)

    tile = 256 if width % 256 == 0 else 128
    tokens = micro_count * rows
    dp_rows = width // dp_count
    own_rows = dp_rows // seq_count
    chunks = 4

    def partial_grads(c):
        if c < 3:
            right = dpk[:, :, c * inner : (c + 1) * inner].reshape(tokens, inner)
            left_ref = nb
        else:
            right = mx[...].reshape(tokens, inner)
            left_ref = gb

        def rows_of(i, carry):
            cols = pl.ds(pl.multiple_of(i * tile, tile), tile)
            left = left_ref[:, :, cols].reshape(tokens, tile)
            cw[c, cols, :] = dot(left, right, 0, 0).astype(jnp.bfloat16)
            return carry

        lax.fori_loop(0, width // tile, rows_of, 0)

    def block_rows(x, of_core):
        return pl.ds(pl.multiple_of((2 * x + of_core) * dp_rows, dp_rows), dp_rows)

    def core_copy(c, x):
        return pltpu.make_async_remote_copy(
            src_ref=cw.at[c, block_rows(x, 1 - core), :],
            dst_ref=core_in.at[c, x],
            send_sem=core_send.at[c, x],
            recv_sem=core_recv.at[c, x],
            device_id=other_core,
            device_id_type=MESH,
        )

    def reach(count, c, way):
        return count // 2 if (c + way) % 2 == 0 else count // 2 - 1

    def ring_copy(own, landing, send, recv, c, way, distance, count, me, at):
        step = 1 if way == 0 else -1
        target = lax.rem(me + step * distance + count, count)
        return pltpu.make_async_remote_copy(
            src_ref=own.at[c, target],
            dst_ref=landing.at[c, way, distance - 1],
            send_sem=send.at[c, way, distance - 1],
            recv_sem=recv.at[c, way, distance - 1],
            device_id=at(step),
            device_id_type=MESH,
        )

    def x_copy(c, way, distance):
        return ring_copy(
            xs, x_in, ring_x_send, ring_x_recv, c, way, distance, x_count, x_id, at_x
        )

    def z_copy(c, way, distance):
        return ring_copy(
            zs, z_in, ring_z_send, ring_z_recv, c, way, distance, seq_count, seq_id, at_z
        )

    def ring_step(copy, own, landing, count, me, c, distance):
        for way in range(2):
            limit = reach(count, c, way)
            if distance > limit:
                continue
            if distance < limit:
                copy(c, way, distance + 1).wait_recv()
                step = 1 if way == 0 else -1
                target = lax.rem(me + step * distance + count, count)
                own[c, target] = (
                    own[c, target].astype(jnp.float32)
                    + landing[c, way, distance].astype(jnp.float32)
                ).astype(jnp.bfloat16)
            copy(c, way, distance).start()

    def ring_total(copy, own, landing, count, me, c):
        total = own[c, me].astype(jnp.float32)
        for way in range(2):
            if reach(count, c, way) > 0:
                copy(c, way, 1).wait_recv()
                total = total + landing[c, way, 0].astype(jnp.float32)
        return total

    def start_core(c):
        partial_grads(c)
        for x in range(x_count):
            core_copy(c, x).start()

    def start_x(c):
        for x in range(x_count):
            core_copy(c, x).wait_recv()
            xs[c, x] = (
                cw[c, block_rows(x, core), :].astype(jnp.float32)
                + core_in[c, x].astype(jnp.float32)
            ).astype(jnp.bfloat16)
        ring_step(x_copy, xs, x_in, x_count, x_id, c, x_count // 2)

    def next_x(c, distance):
        ring_step(x_copy, xs, x_in, x_count, x_id, c, distance)

    def start_z(c):
        block_sum[...] = ring_total(x_copy, xs, x_in, x_count, x_id, c)
        for k in range(seq_count):
            zs[c, k] = block_sum[k * own_rows : (k + 1) * own_rows, :].astype(jnp.bfloat16)
        ring_step(z_copy, zs, z_in, seq_count, seq_id, c, seq_count // 2)

    def next_z(c, distance):
        ring_step(z_copy, zs, z_in, seq_count, seq_id, c, distance)

    def finish(c):
        total = ring_total(z_copy, zs, z_in, seq_count, seq_id, c)
        if c < 3:
            grad_qkv_ref[:, c * inner : (c + 1) * inner] = total
        else:
            grad_out_ref[...] = total

    stages = [start_core, start_x]
    stages += [functools.partial(next_x, distance=d) for d in range(x_count // 2 - 1, 0, -1)]
    stages += [start_z]
    stages += [functools.partial(next_z, distance=d) for d in range(seq_count // 2 - 1, 0, -1)]
    stages += [finish]
    for tick in range(chunks + len(stages) - 1):
        for c in range(chunks):
            if 0 <= tick - c < len(stages):
                stages[tick - c](c)

    for c in range(chunks):
        for x in range(x_count):
            core_copy(c, x).wait_send()
        for way in range(2):
            for d in range(1, reach(x_count, c, way) + 1):
                x_copy(c, way, d).wait_send()
            for d in range(1, reach(seq_count, c, way) + 1):
                z_copy(c, way, d).wait_send()

    for m in range(micro_count):

        @pl.when(section < section_count - 1)
        def _():
            for k in range(seq_count):
                hop(hb, xb, x_send, x_recv, m, k, 1).wait_send()

        @pl.when(section > 0)
        def _():
            for k in range(seq_count):
                hop(bb, gb, g_send, g_recv, m, k, -1).wait_send()

        @pl.when(is_odd)
        def _():
            output_back(m).wait_send()
            output_own(m).wait()

        @pl.when(jnp.logical_not(is_odd))
        def _():
            pltpu.make_async_copy(out_hbm.at[m], out_hbm.at[m], o_recv.at[m]).wait()


def relay(seq_count, section_count, x, w_qkv, w_out, g):
    micro_count, rows, width = x.shape
    inner = w_out.shape[0]
    pairs = inner // (2 * HEAD_DIM)
    bf16, f32 = jnp.bfloat16, jnp.float32
    tokens = (micro_count, rows, width)
    dma = pltpu.SemaphoreType.DMA
    dp_count = lax.axis_size("dp")
    x_count = dp_count // 2
    dp_rows = width // dp_count
    own_rows = dp_rows // seq_count
    any_spec = pl.BlockSpec(memory_space=pl.ANY)
    vmem_spec = pl.BlockSpec(memory_space=pltpu.VMEM)
    return pl.pallas_call(
        functools.partial(relay_kernel, seq_count, section_count),
        out_shape=(
            jax.ShapeDtypeStruct(tokens, bf16),
            jax.ShapeDtypeStruct((own_rows, 3 * inner), f32),
            jax.ShapeDtypeStruct((own_rows, inner), f32),
        ),
        in_specs=[any_spec] * 4,
        out_specs=(any_spec, vmem_spec, vmem_spec),
        scratch_shapes=[
            pltpu.VMEM((width, 3 * inner), bf16),
            pltpu.VMEM((inner, width), bf16),
            pltpu.VMEM(tokens, bf16),
            pltpu.VMEM(tokens, bf16),
            pltpu.VMEM(tokens, f32),
            pltpu.VMEM((micro_count, rows, 128), f32),
            pltpu.VMEM(tokens, bf16),
            pltpu.VMEM((micro_count, rows, 3 * inner), bf16),
            pltpu.VMEM((micro_count, pairs, 2 * rows, rows), f32),
            pltpu.VMEM((micro_count, rows, inner), bf16),
            pltpu.VMEM((micro_count, rows, 3 * inner), bf16),
            pltpu.VMEM(tokens, bf16),
            pltpu.VMEM(tokens, bf16),
            dma((4,)),
            dma((micro_count, seq_count)),
            dma((micro_count, seq_count)),
            dma((micro_count, seq_count)),
            dma((micro_count, seq_count)),
            dma((micro_count,)),
            dma((micro_count,)),
            pltpu.VMEM((4, width, inner), bf16),
            pltpu.VMEM((4, x_count, dp_rows, inner), bf16),
            pltpu.VMEM((4, x_count, dp_rows, inner), bf16),
            pltpu.VMEM((4, 2, x_count // 2, dp_rows, inner), bf16),
            pltpu.VMEM((dp_rows, inner), f32),
            pltpu.VMEM((4, seq_count, own_rows, inner), bf16),
            pltpu.VMEM((4, 2, seq_count // 2, own_rows, inner), bf16),
            dma((4, x_count)),
            dma((4, x_count)),
            dma((4, 2, x_count // 2)),
            dma((4, 2, x_count // 2)),
            dma((4, 2, seq_count // 2)),
            dma((4, 2, seq_count // 2)),
        ],
        compiler_params=pltpu.CompilerParams(
            collective_id=0, has_side_effects=True, vmem_limit_bytes=60 * 1024 * 1024
        ),
        name="relay",
    )(x, w_qkv, w_out, g)


def local(clips_in, w_qkv, w_out, out_cotangent):
    seq_count = lax.axis_size("seq")
    section_count = lax.axis_size("section")
    micro_count, frames, patches_dev, width = clips_in.shape
    x = clips_in.reshape(micro_count, frames * patches_dev, width)
    g = out_cotangent.reshape(micro_count, -1, width)
    outputs, grad_qkv, grad_out = relay(seq_count, section_count, x, w_qkv[0], w_out[0], g)
    return (outputs.reshape((1,) + out_cotangent.shape), grad_qkv[None], grad_out[None])


def solution(mesh):
    return jax.shard_map(
        local,
        mesh=mesh,
        in_specs=(
            P("dp", None, "seq", None),
            P("section", None, None),
            P("section", None, None),
            P("dp", "seq", None, None),
        ),
        out_specs=(
            P("section", "dp", "seq", None, None),
            P("section", ("dp", "seq"), None),
            P("section", ("dp", "seq"), None),
        ),
        check_vma=False,
    )
```

```python
import functools
import math

import jax
import jax.numpy as jnp
from jax import lax
from jax.experimental import pallas as pl
from jax.experimental.pallas import tpu as pltpu
from jax.sharding import PartitionSpec as P

HEAD_DIM = 64
NORM_EPS = 1e-05
MASKED = -1e30
MESH = pl.DeviceIdType.MESH


def dot(a, b, a_dim, b_dim):
    return lax.dot_general(
        a, b, (((a_dim,), (b_dim,)), ((), ())), preferred_element_type=jnp.float32
    )


def relay_kernel(
    seq_count,
    section_count,
    x_hbm,
    w_qkv_hbm,
    w_out_hbm,
    g_hbm,
    out_hbm,
    grad_qkv_ref,
    grad_out_ref,
    wq,
    wo,
    xb,
    gb,
    ub,
    rb,
    nb,
    pk,
    pr,
    mx,
    dpk,
    hb,
    bb,
    in_sem,
    x_send,
    x_recv,
    g_send,
    g_recv,
    o_send,
    o_recv,
    cw,
    core_in,
    xs,
    x_in,
    block_sum,
    zs,
    z_in,
    core_send,
    core_recv,
    ring_x_send,
    ring_x_recv,
    ring_z_send,
    ring_z_recv,
    turn,
):
    dp_id = lax.axis_index("dp")
    section = lax.axis_index("section")
    seq_id = lax.axis_index("seq")
    micro_count, rows, width = xb.shape
    block = rows // seq_count
    inner = wo.shape[0]
    pairs = inner // (2 * HEAD_DIM)
    scale = 1.0 / math.sqrt(HEAD_DIM)
    dp_count = lax.axis_size("dp")
    x_count = dp_count // 2
    x_id = dp_id // 2
    core = lax.rem(dp_id, 2)
    is_first = section == 0
    is_last = section == section_count - 1
    is_odd = lax.rem(section, 2) == 1

    load_wq = pltpu.make_async_copy(w_qkv_hbm, wq, in_sem.at[0])
    load_wo = pltpu.make_async_copy(w_out_hbm, wo, in_sem.at[1])
    load_x = pltpu.make_async_copy(x_hbm, xb, in_sem.at[2])
    load_g = pltpu.make_async_copy(g_hbm, gb, in_sem.at[3])

    @pl.when(is_first)
    def _():
        load_x.start()

    load_wq.start()
    load_wo.start()

    @pl.when(is_last)
    def _():
        load_g.start()

    barrier = pltpu.get_barrier_semaphore()

    @pl.when(section > 0)
    def _():
        for k in range(seq_count):
            pl.semaphore_signal(
                barrier, inc=1, device_id=(dp_id, section - 1, k), device_id_type=MESH
            )

    @pl.when(section < section_count - 1)
    def _():
        for k in range(seq_count):
            pl.semaphore_signal(
                barrier, inc=1, device_id=(dp_id, section + 1, k), device_id_type=MESH
            )

    def at_x(step):
        return (2 * lax.rem(x_id + step + x_count, x_count) + core, section, seq_id)

    def at_z(step):
        return (dp_id, section, lax.rem(seq_id + step + seq_count, seq_count))

    other_core = (2 * x_id + 1 - core, section, seq_id)
    for peer in (other_core, at_x(1), at_x(-1), at_z(1), at_z(-1)):
        pl.semaphore_signal(barrier, inc=1, device_id=peer, device_id_type=MESH)
    inner_section = jnp.logical_and(section > 0, section < section_count - 1)
    pl.semaphore_wait(barrier, jnp.where(inner_section, 2 * seq_count + 5, seq_count + 5))

    def hop(src, dst, send, recv, m, k, step):
        return pltpu.make_async_remote_copy(
            src_ref=src.at[m, pl.ds(k * block, block), :],
            dst_ref=dst.at[m, pl.ds(seq_id * block, block), :],
            send_sem=send.at[m, k],
            recv_sem=recv.at[m, seq_id],
            device_id=(dp_id, section + step, k),
            device_id_type=MESH,
        )

    def arrival(dst, recv, m, k):
        landed = dst.at[m, pl.ds(k * block, block), :]
        return pltpu.make_async_copy(landed, landed, recv.at[m, k])

    def output_back(m):
        return pltpu.make_async_remote_copy(
            src_ref=xb.at[m],
            dst_ref=out_hbm.at[m],
            send_sem=o_send.at[m],
            recv_sem=o_recv.at[m],
            device_id=(dp_id, section - 1, seq_id),
            device_id_type=MESH,
        )

    def output_own(m):
        return pltpu.make_async_copy(hb.at[m], out_hbm.at[m], o_recv.at[m])

    lane = lax.broadcasted_iota(jnp.int32, (rows, 2 * HEAD_DIM), 1)
    first_head = lane < HEAD_DIM
    row_group = lax.rem(lax.broadcasted_iota(jnp.int32, (2 * rows, rows), 0), block)
    col_group = lax.rem(lax.broadcasted_iota(jnp.int32, (2 * rows, rows), 1), block)
    same_group = jnp.where(row_group == col_group, 1, 0) + jnp.where(is_odd, 1, 0) > 0

    def stacked(part):
        zero = jnp.zeros_like(part)
        return jnp.concatenate(
            [jnp.where(first_head, part, zero), jnp.where(first_head, zero, part)], axis=0
        )

    def joined(part):
        return jnp.where(first_head, part[:rows], part[rows:])

    def start_forward(m):
        for k in range(seq_count):
            hop(hb, xb, x_send, x_recv, m, k, 1).start()

    def sent_forward(m, first, last):
        for k in range(first, last):
            hop(hb, xb, x_send, x_recv, m, k, 1).wait_send()

    def send_in_turns():
        early = (3 * seq_count) // 4
        for m in range(micro_count):
            for c in range(2):
                turn_id = 2 * m + c

                @pl.when(core == c)
                def _():
                    if turn_id > 0:
                        pl.semaphore_wait(turn.at[turn_id - 1], 1)
                        start_forward(m)
                    sent_forward(m, 0, early)
                    if turn_id < 2 * micro_count - 1:
                        pl.semaphore_signal(
                            turn.at[turn_id], inc=1, device_id=other_core, device_id_type=MESH
                        )
                    sent_forward(m, early, seq_count)

    def forward(m):
        @pl.when(section > 0)
        def _():
            for k in range(seq_count):
                arrival(xb, x_recv, m, k).wait()

        values = xb[m].astype(jnp.float32)
        centred = values - jnp.mean(values, axis=-1, keepdims=True)
        inverse = lax.rsqrt(jnp.mean(centred * centred, axis=-1, keepdims=True) + NORM_EPS)
        unit = centred * inverse
        ub[m] = unit
        rb[m] = jnp.broadcast_to(inverse, (rows, 128))
        nb[m] = unit.astype(jnp.bfloat16)
        pk[m] = dot(nb[m], wq[...], 1, 0).astype(jnp.bfloat16)
        for p in range(pairs):
            cols = pl.ds(p * 128, 128)
            query = pk[m, :, pl.ds(p * 128, 128)]
            key = pk[m, :, pl.ds(inner + p * 128, 128)]
            value = pk[m, :, pl.ds(2 * inner + p * 128, 128)]
            scores = dot(stacked(query), key, 1, 1) * scale
            scores = jnp.where(same_group, scores, MASKED)
            exps = jnp.exp(scores - jnp.max(scores, axis=-1, keepdims=True))
            probs = exps / jnp.sum(exps, axis=-1, keepdims=True)
            pr[m, p] = probs
            mx[m, :, cols] = joined(dot(probs.astype(jnp.bfloat16), value, 1, 0)).astype(
                jnp.bfloat16
            )
        hb[m] = (xb[m].astype(jnp.float32) + dot(mx[m], wo[...], 1, 0)).astype(jnp.bfloat16)

        @pl.when(jnp.logical_and(section > 0, section < section_count - 1))
        def _():
            start_forward(m)

        @pl.when(jnp.logical_and(is_first, core + m == 0))
        def _():
            start_forward(0)

        @pl.when(jnp.logical_and(is_first, m == micro_count - 1))
        def _():
            send_in_turns()

        @pl.when(is_odd)
        def _():
            output_own(m).start()

    def backward(m):
        @pl.when(section < section_count - 1)
        def _():
            for k in range(seq_count):
                arrival(gb, g_recv, m, k).wait()

        d_mixed = dot(gb[m], wo[...], 1, 1).astype(jnp.bfloat16)
        for p in range(pairs):
            query = stacked(pk[m, :, pl.ds(p * 128, 128)])
            key = pk[m, :, pl.ds(inner + p * 128, 128)]
            value = pk[m, :, pl.ds(2 * inner + p * 128, 128)]
            d_heads = stacked(d_mixed[:, p * 128 : (p + 1) * 128])
            probs = pr[m, p]
            d_values = dot(probs.astype(jnp.bfloat16), d_heads, 0, 0)
            d_probs = dot(d_heads, value, 1, 1)
            d_scores = probs * (d_probs - jnp.sum(probs * d_probs, axis=-1, keepdims=True))
            d_scores = d_scores.astype(jnp.bfloat16)
            d_query = joined(dot(d_scores, key, 1, 0)) * scale
            d_keys = dot(d_scores, query, 0, 0) * scale
            dpk[m, :, pl.ds(p * 128, 128)] = d_query.astype(jnp.bfloat16)
            dpk[m, :, pl.ds(inner + p * 128, 128)] = d_keys.astype(jnp.bfloat16)
            dpk[m, :, pl.ds(2 * inner + p * 128, 128)] = d_values.astype(jnp.bfloat16)

        @pl.when(section > 0)
        def _():
            d_normed = dot(dpk[m], wq[...], 1, 1)
            unit = ub[m]
            d_inside = rb[m, :, 0:1] * (
                d_normed
                - jnp.mean(d_normed, axis=-1, keepdims=True)
                - unit * jnp.mean(d_normed * unit, axis=-1, keepdims=True)
            )
            bb[m] = (gb[m].astype(jnp.float32) + d_inside).astype(jnp.bfloat16)
            for k in range(seq_count):
                hop(bb, gb, g_send, g_recv, m, k, -1).start()

    @pl.when(is_first)
    def _():
        load_x.wait()

    load_wq.wait()
    load_wo.wait()

    @pl.when(is_last)
    def _():
        load_g.wait()

    def step(t, carry):
        m = jnp.where(is_last, t // 2, lax.rem(t, micro_count))
        back = jnp.where(is_last, lax.rem(t, 2), t // micro_count)

        @pl.when(back == 0)
        def _():
            forward(m)

        @pl.when(back == 1)
        def _():
            backward(m)

        return carry

    lax.fori_loop(0, 2 * micro_count, step, 0)

    @pl.when(is_odd)
    def _():
        for m in range(micro_count):
            output_back(m).start()

    tile = 256 if width % 256 == 0 else 128
    tokens = micro_count * rows
    dp_rows = width // dp_count
    own_rows = dp_rows // seq_count
    chunks = 4

    def partial_grads(c):
        if c < 3:
            right = dpk[:, :, c * inner : (c + 1) * inner].reshape(tokens, inner)
            left_ref = nb
        else:
            right = mx[...].reshape(tokens, inner)
            left_ref = gb

        def rows_of(i, carry):
            cols = pl.ds(pl.multiple_of(i * tile, tile), tile)
            left = left_ref[:, :, cols].reshape(tokens, tile)
            cw[c, cols, :] = dot(left, right, 0, 0).astype(jnp.bfloat16)
            return carry

        lax.fori_loop(0, width // tile, rows_of, 0)

    def block_rows(x, of_core):
        return pl.ds(pl.multiple_of((2 * x + of_core) * dp_rows, dp_rows), dp_rows)

    def core_copy(c, x):
        return pltpu.make_async_remote_copy(
            src_ref=cw.at[c, block_rows(x, 1 - core), :],
            dst_ref=core_in.at[c, x],
            send_sem=core_send.at[c, x],
            recv_sem=core_recv.at[c, x],
            device_id=other_core,
            device_id_type=MESH,
        )

    def reach(count, c, way, halved):
        return count // 2 if halved or (c + way) % 2 == 0 else count // 2 - 1

    def extent(count, way, distance, halved, size):
        if halved and distance == count // 2:
            return pl.ds(way * (size // 2), size // 2)
        return pl.ds(0, size)

    def ring_copy(own, landing, send, recv, c, way, distance, count, me, at, halved):
        step = 1 if way == 0 else -1
        target = lax.rem(me + step * distance + count, count)
        part = extent(count, way, distance, halved, own.shape[2])
        return pltpu.make_async_remote_copy(
            src_ref=own.at[c, target, part, :],
            dst_ref=landing.at[c, way, distance - 1, part, :],
            send_sem=send.at[c, way, distance - 1],
            recv_sem=recv.at[c, way, distance - 1],
            device_id=at(step),
            device_id_type=MESH,
        )

    def x_copy(c, way, distance):
        return ring_copy(
            xs, x_in, ring_x_send, ring_x_recv, c, way, distance, x_count, x_id, at_x, True
        )

    def z_copy(c, way, distance):
        return ring_copy(
            zs, z_in, ring_z_send, ring_z_recv, c, way, distance, seq_count, seq_id, at_z, False
        )

    def ring_step(copy, own, landing, count, me, c, distance, halved):
        for way in range(2):
            limit = reach(count, c, way, halved)
            if distance > limit:
                continue
            if distance < limit:
                copy(c, way, distance + 1).wait_recv()
                step = 1 if way == 0 else -1
                target = lax.rem(me + step * distance + count, count)
                part = extent(count, way, distance + 1, halved, own.shape[2])
                own[c, target, part, :] = (
                    own[c, target, part, :].astype(jnp.float32)
                    + landing[c, way, distance, part, :].astype(jnp.float32)
                ).astype(jnp.bfloat16)
            copy(c, way, distance).start()

    def ring_total(copy, own, landing, count, me, c, halved):
        total = own[c, me].astype(jnp.float32)
        for way in range(2):
            if reach(count, c, way, halved) > 0:
                copy(c, way, 1).wait_recv()
                total = total + landing[c, way, 0].astype(jnp.float32)
        return total

    def start_core(c):
        partial_grads(c)
        for x in range(x_count):
            core_copy(c, x).start()

    def start_x(c):
        for x in range(x_count):
            core_copy(c, x).wait_recv()
            xs[c, x] = (
                cw[c, block_rows(x, core), :].astype(jnp.float32)
                + core_in[c, x].astype(jnp.float32)
            ).astype(jnp.bfloat16)
        ring_step(x_copy, xs, x_in, x_count, x_id, c, x_count // 2, True)

    def next_x(c, distance):
        ring_step(x_copy, xs, x_in, x_count, x_id, c, distance, True)

    def start_z(c):
        block_sum[...] = ring_total(x_copy, xs, x_in, x_count, x_id, c, True)
        for k in range(seq_count):
            zs[c, k] = block_sum[k * own_rows : (k + 1) * own_rows, :].astype(jnp.bfloat16)
        ring_step(z_copy, zs, z_in, seq_count, seq_id, c, seq_count // 2, False)

    def next_z(c, distance):
        ring_step(z_copy, zs, z_in, seq_count, seq_id, c, distance, False)

    def finish(c):
        total = ring_total(z_copy, zs, z_in, seq_count, seq_id, c, False)
        if c < 3:
            grad_qkv_ref[:, c * inner : (c + 1) * inner] = total
        else:
            grad_out_ref[...] = total

    stages = [start_core, start_x]
    stages += [functools.partial(next_x, distance=d) for d in range(x_count // 2 - 1, 0, -1)]
    stages += [start_z]
    stages += [functools.partial(next_z, distance=d) for d in range(seq_count // 2 - 1, 0, -1)]
    stages += [finish]
    for tick in range(chunks + len(stages) - 1):
        for c in range(chunks):
            if 0 <= tick - c < len(stages):
                stages[tick - c](c)

    for c in range(chunks):
        for x in range(x_count):
            core_copy(c, x).wait_send()
        for way in range(2):
            for d in range(1, reach(x_count, c, way, True) + 1):
                x_copy(c, way, d).wait_send()
            for d in range(1, reach(seq_count, c, way, False) + 1):
                z_copy(c, way, d).wait_send()

    for m in range(micro_count):

        @pl.when(jnp.logical_and(section > 0, section < section_count - 1))
        def _():
            sent_forward(m, 0, seq_count)

        @pl.when(section > 0)
        def _():
            for k in range(seq_count):
                hop(bb, gb, g_send, g_recv, m, k, -1).wait_send()

        @pl.when(is_odd)
        def _():
            output_back(m).wait_send()
            output_own(m).wait()

        @pl.when(jnp.logical_not(is_odd))
        def _():
            pltpu.make_async_copy(out_hbm.at[m], out_hbm.at[m], o_recv.at[m]).wait()


def relay(seq_count, section_count, x, w_qkv, w_out, g):
    micro_count, rows, width = x.shape
    inner = w_out.shape[0]
    pairs = inner // (2 * HEAD_DIM)
    bf16, f32 = jnp.bfloat16, jnp.float32
    tokens = (micro_count, rows, width)
    dma = pltpu.SemaphoreType.DMA
    dp_count = lax.axis_size("dp")
    x_count = dp_count // 2
    dp_rows = width // dp_count
    own_rows = dp_rows // seq_count
    any_spec = pl.BlockSpec(memory_space=pl.ANY)
    vmem_spec = pl.BlockSpec(memory_space=pltpu.VMEM)
    return pl.pallas_call(
        functools.partial(relay_kernel, seq_count, section_count),
        out_shape=(
            jax.ShapeDtypeStruct(tokens, bf16),
            jax.ShapeDtypeStruct((own_rows, 3 * inner), f32),
            jax.ShapeDtypeStruct((own_rows, inner), f32),
        ),
        in_specs=[any_spec] * 4,
        out_specs=(any_spec, vmem_spec, vmem_spec),
        scratch_shapes=[
            pltpu.VMEM((width, 3 * inner), bf16),
            pltpu.VMEM((inner, width), bf16),
            pltpu.VMEM(tokens, bf16),
            pltpu.VMEM(tokens, bf16),
            pltpu.VMEM(tokens, f32),
            pltpu.VMEM((micro_count, rows, 128), f32),
            pltpu.VMEM(tokens, bf16),
            pltpu.VMEM((micro_count, rows, 3 * inner), bf16),
            pltpu.VMEM((micro_count, pairs, 2 * rows, rows), f32),
            pltpu.VMEM((micro_count, rows, inner), bf16),
            pltpu.VMEM((micro_count, rows, 3 * inner), bf16),
            pltpu.VMEM(tokens, bf16),
            pltpu.VMEM(tokens, bf16),
            dma((4,)),
            dma((micro_count, seq_count)),
            dma((micro_count, seq_count)),
            dma((micro_count, seq_count)),
            dma((micro_count, seq_count)),
            dma((micro_count,)),
            dma((micro_count,)),
            pltpu.VMEM((4, width, inner), bf16),
            pltpu.VMEM((4, x_count, dp_rows, inner), bf16),
            pltpu.VMEM((4, x_count, dp_rows, inner), bf16),
            pltpu.VMEM((4, 2, x_count // 2, dp_rows, inner), bf16),
            pltpu.VMEM((dp_rows, inner), f32),
            pltpu.VMEM((4, seq_count, own_rows, inner), bf16),
            pltpu.VMEM((4, 2, seq_count // 2, own_rows, inner), bf16),
            dma((4, x_count)),
            dma((4, x_count)),
            dma((4, 2, x_count // 2)),
            dma((4, 2, x_count // 2)),
            dma((4, 2, seq_count // 2)),
            dma((4, 2, seq_count // 2)),
            pltpu.SemaphoreType.REGULAR((2 * micro_count,)),
        ],
        compiler_params=pltpu.CompilerParams(
            collective_id=0, has_side_effects=True, vmem_limit_bytes=60 * 1024 * 1024
        ),
        name="relay",
    )(x, w_qkv, w_out, g)


def local(clips_in, w_qkv, w_out, out_cotangent):
    seq_count = lax.axis_size("seq")
    section_count = lax.axis_size("section")
    micro_count, frames, patches_dev, width = clips_in.shape
    x = clips_in.reshape(micro_count, frames * patches_dev, width)
    g = out_cotangent.reshape(micro_count, -1, width)
    outputs, grad_qkv, grad_out = relay(seq_count, section_count, x, w_qkv[0], w_out[0], g)
    return (outputs.reshape((1,) + out_cotangent.shape), grad_qkv[None], grad_out[None])


def solution(mesh):
    return jax.shard_map(
        local,
        mesh=mesh,
        in_specs=(
            P("dp", None, "seq", None),
            P("section", None, None),
            P("section", None, None),
            P("dp", "seq", None, None),
        ),
        out_specs=(
            P("section", "dp", "seq", None, None),
            P("section", ("dp", "seq"), None),
            P("section", ("dp", "seq"), None),
        ),
        check_vma=False,
    )
```

```python
import functools
import math

import jax
import jax.numpy as jnp
from jax import lax
from jax.experimental import pallas as pl
from jax.experimental.pallas import tpu as pltpu
from jax.sharding import PartitionSpec as P

HEAD_DIM = 64
NORM_EPS = 1e-05
MASKED = -1e30
MESH = pl.DeviceIdType.MESH


def dot(a, b, a_dim, b_dim):
    return lax.dot_general(
        a, b, (((a_dim,), (b_dim,)), ((), ())), preferred_element_type=jnp.float32
    )


def relay_kernel(
    seq_count,
    section_count,
    x_hbm,
    w_qkv_hbm,
    w_out_hbm,
    g_hbm,
    out_hbm,
    grad_qkv_ref,
    grad_out_ref,
    wq,
    wo,
    xb,
    gb,
    ub,
    rb,
    nb,
    pk,
    pr,
    mx,
    dpk,
    hb,
    bb,
    in_sem,
    x_send,
    x_recv,
    g_send,
    g_recv,
    o_send,
    o_recv,
    cw,
    core_in,
    xs,
    x_in,
    block_sum,
    zs,
    z_in,
    core_send,
    core_recv,
    ring_x_send,
    ring_x_recv,
    z_send,
    z_recv,
    turn,
    wqt,
    wot,
):
    dp_id = lax.axis_index("dp")
    section = lax.axis_index("section")
    seq_id = lax.axis_index("seq")
    micro_count, rows, width = xb.shape
    block = rows // seq_count
    inner = wo.shape[0]
    pairs = inner // (2 * HEAD_DIM)
    scale = 1.0 / math.sqrt(HEAD_DIM)
    dp_count = lax.axis_size("dp")
    x_count = dp_count // 2
    x_id = dp_id // 2
    core = lax.rem(dp_id, 2)
    is_first = section == 0
    is_last = section == section_count - 1
    is_odd = lax.rem(section, 2) == 1

    load_wq = pltpu.make_async_copy(w_qkv_hbm, wq, in_sem.at[0])
    load_wo = pltpu.make_async_copy(w_out_hbm, wo, in_sem.at[1])
    load_x = pltpu.make_async_copy(x_hbm, xb, in_sem.at[2])
    load_g = pltpu.make_async_copy(g_hbm, gb, in_sem.at[3])

    @pl.when(is_first)
    def _():
        load_x.start()

    load_wq.start()
    load_wo.start()

    @pl.when(is_last)
    def _():
        load_g.start()

    barrier = pltpu.get_barrier_semaphore()

    @pl.when(section > 0)
    def _():
        for k in range(seq_count):
            pl.semaphore_signal(
                barrier, inc=1, device_id=(dp_id, section - 1, k), device_id_type=MESH
            )

    @pl.when(section < section_count - 1)
    def _():
        for k in range(seq_count):
            pl.semaphore_signal(
                barrier, inc=1, device_id=(dp_id, section + 1, k), device_id_type=MESH
            )

    def at_x(step):
        return (2 * lax.rem(x_id + step + x_count, x_count) + core, section, seq_id)

    def at_z(step):
        return (dp_id, section, lax.rem(seq_id + step + seq_count, seq_count))

    other_core = (2 * x_id + 1 - core, section, seq_id)
    peers = [other_core, at_x(1), at_x(-1)] + [at_z(step) for step in range(1, seq_count)]
    for peer in peers:
        pl.semaphore_signal(barrier, inc=1, device_id=peer, device_id_type=MESH)

    def wait_for_peers():
        inner_section = jnp.logical_and(section > 0, section < section_count - 1)
        hops = jnp.where(inner_section, 2 * seq_count, seq_count)
        pl.semaphore_wait(barrier, hops + len(peers))


    def hop(src, dst, send, recv, m, k, step):
        return pltpu.make_async_remote_copy(
            src_ref=src.at[m, pl.ds(k * block, block), :],
            dst_ref=dst.at[m, pl.ds(seq_id * block, block), :],
            send_sem=send.at[m, k],
            recv_sem=recv.at[m, seq_id],
            device_id=(dp_id, section + step, k),
            device_id_type=MESH,
        )

    def arrival(dst, recv, m, k):
        landed = dst.at[m, pl.ds(k * block, block), :]
        return pltpu.make_async_copy(landed, landed, recv.at[m, k])

    def output_back(m):
        return pltpu.make_async_remote_copy(
            src_ref=xb.at[m],
            dst_ref=out_hbm.at[m],
            send_sem=o_send.at[m],
            recv_sem=o_recv.at[m],
            device_id=(dp_id, section - 1, seq_id),
            device_id_type=MESH,
        )

    def output_own(m):
        return pltpu.make_async_copy(hb.at[m], out_hbm.at[m], o_recv.at[m])

    lane = lax.broadcasted_iota(jnp.int32, (rows, 2 * HEAD_DIM), 1)
    first_head = lane < HEAD_DIM
    row_group = lax.rem(lax.broadcasted_iota(jnp.int32, (2 * rows, rows), 0), block)
    col_group = lax.rem(lax.broadcasted_iota(jnp.int32, (2 * rows, rows), 1), block)
    same_group = jnp.where(row_group == col_group, 1, 0) + jnp.where(is_odd, 1, 0) > 0

    def stacked(part):
        zero = jnp.zeros_like(part)
        return jnp.concatenate(
            [jnp.where(first_head, part, zero), jnp.where(first_head, zero, part)], axis=0
        )

    def joined(part):
        return jnp.where(first_head, part[:rows], part[rows:])

    tile = 256 if width % 256 == 0 else 128
    tokens = micro_count * rows
    dp_rows = width // dp_count
    own_rows = dp_rows // seq_count
    chunks = 4

    def partial_grads(c):
        if c < 3:
            right = dpk[:, :, c * inner : (c + 1) * inner].reshape(tokens, inner)
            left_ref = nb
        else:
            right = mx[...].reshape(tokens, inner)
            left_ref = gb

        def rows_of(i, carry):
            cols = pl.ds(pl.multiple_of(i * tile, tile), tile)
            left = left_ref[:, :, cols].reshape(tokens, tile)
            cw[c, cols, :] = dot(left, right, 0, 0).astype(jnp.bfloat16)
            return carry

        lax.fori_loop(0, width // tile, rows_of, 0)

    def block_rows(x, of_core):
        return pl.ds(pl.multiple_of((2 * x + of_core) * dp_rows, dp_rows), dp_rows)

    def core_copy(c, x):
        return pltpu.make_async_remote_copy(
            src_ref=cw.at[c, block_rows(x, 1 - core), :],
            dst_ref=core_in.at[c, x],
            send_sem=core_send.at[c, x],
            recv_sem=core_recv.at[c, x],
            device_id=other_core,
            device_id_type=MESH,
        )

    def start_core(c):
        partial_grads(c)
        for x in range(x_count):
            core_copy(c, x).start()

    def start_forward(m):
        for k in range(seq_count):
            hop(hb, xb, x_send, x_recv, m, k, 1).start()

    def sent_forward(m, first, last):
        for k in range(first, last):
            hop(hb, xb, x_send, x_recv, m, k, 1).wait_send()

    def send_in_turns():
        early = (3 * seq_count) // 4
        for m in range(micro_count):
            for c in range(2):
                turn_id = 2 * m + c

                @pl.when(core == c)
                def _():
                    if turn_id > 0:
                        pl.semaphore_wait(turn.at[turn_id - 1], 1)
                        start_forward(m)
                    sent_forward(m, 0, early)
                    if turn_id < 2 * micro_count - 1:
                        pl.semaphore_signal(
                            turn.at[turn_id], inc=1, device_id=other_core, device_id_type=MESH
                        )
                    sent_forward(m, early, seq_count)

    def forward(m):
        @pl.when(section > 0)
        def _():
            for k in range(seq_count):
                arrival(xb, x_recv, m, k).wait()

        values = xb[m].astype(jnp.float32)
        centred = values - jnp.mean(values, axis=-1, keepdims=True)
        inverse = lax.rsqrt(jnp.mean(centred * centred, axis=-1, keepdims=True) + NORM_EPS)
        unit = centred * inverse
        ub[m] = unit
        rb[m] = jnp.broadcast_to(inverse, (rows, 128))
        nb[m] = unit.astype(jnp.bfloat16)
        pk[m] = dot(nb[m], wq[...], 1, 0).astype(jnp.bfloat16)
        for p in range(pairs):
            cols = pl.ds(p * 128, 128)
            query = pk[m, :, pl.ds(p * 128, 128)]
            key = pk[m, :, pl.ds(inner + p * 128, 128)]
            value = pk[m, :, pl.ds(2 * inner + p * 128, 128)]
            scores = dot(stacked(query), key, 1, 1) * scale
            scores = jnp.where(same_group, scores, MASKED)
            exps = jnp.exp(scores - jnp.max(scores, axis=-1, keepdims=True))
            probs = exps / jnp.sum(exps, axis=-1, keepdims=True)
            pr[m, p] = probs
            mx[m, :, cols] = joined(dot(probs.astype(jnp.bfloat16), value, 1, 0)).astype(
                jnp.bfloat16
            )
        hb[m] = (xb[m].astype(jnp.float32) + dot(mx[m], wo[...], 1, 0)).astype(jnp.bfloat16)

        @pl.when(m == 0)
        def _():
            wait_for_peers()

        @pl.when(jnp.logical_and(section > 0, section < section_count - 1))
        def _():
            start_forward(m)

        @pl.when(jnp.logical_and(is_first, core + m == 0))
        def _():
            start_forward(0)

        @pl.when(jnp.logical_and(is_first, m == micro_count - 1))
        def _():
            send_in_turns()

        @pl.when(is_odd)
        def _():
            output_own(m).start()

    def backward(m):
        @pl.when(section < section_count - 1)
        def _():
            for k in range(seq_count):
                arrival(gb, g_recv, m, k).wait()

        @pl.when(jnp.logical_and(is_first, m == micro_count - 1))
        def _():
            start_core(3)

        d_mixed = dot(gb[m], wot[...], 1, 0).astype(jnp.bfloat16)
        for p in range(pairs):
            query = stacked(pk[m, :, pl.ds(p * 128, 128)])
            key = pk[m, :, pl.ds(inner + p * 128, 128)]
            value = pk[m, :, pl.ds(2 * inner + p * 128, 128)]
            d_heads = stacked(d_mixed[:, p * 128 : (p + 1) * 128])
            probs = pr[m, p]
            d_values = dot(probs.astype(jnp.bfloat16), d_heads, 0, 0)
            d_probs = dot(d_heads, value, 1, 1)
            d_scores = probs * (d_probs - jnp.sum(probs * d_probs, axis=-1, keepdims=True))
            d_scores = d_scores.astype(jnp.bfloat16)
            d_query = joined(dot(d_scores, key, 1, 0)) * scale
            d_keys = dot(d_scores, query, 0, 0) * scale
            dpk[m, :, pl.ds(p * 128, 128)] = d_query.astype(jnp.bfloat16)
            dpk[m, :, pl.ds(inner + p * 128, 128)] = d_keys.astype(jnp.bfloat16)
            dpk[m, :, pl.ds(2 * inner + p * 128, 128)] = d_values.astype(jnp.bfloat16)

        @pl.when(section > 0)
        def _():
            d_normed = dot(dpk[m], wqt[...], 1, 0)
            unit = ub[m]
            d_inside = rb[m, :, 0:1] * (
                d_normed
                - jnp.mean(d_normed, axis=-1, keepdims=True)
                - unit * jnp.mean(d_normed * unit, axis=-1, keepdims=True)
            )
            bb[m] = (gb[m].astype(jnp.float32) + d_inside).astype(jnp.bfloat16)
            for k in range(seq_count):
                hop(bb, gb, g_send, g_recv, m, k, -1).start()

    @pl.when(is_first)
    def _():
        load_x.wait()

    load_wq.wait()
    load_wo.wait()

    @pl.when(is_last)
    def _():
        load_g.wait()

    def transpose_weights():
        def part(i, carry):
            cols = pl.ds(pl.multiple_of(i * 128, 128), 128)
            wqt[cols, :] = wq[:, cols].T
            return carry

        @pl.when(section > 0)
        def _():
            lax.fori_loop(0, 3 * inner // 128, part, 0)

        def out_part(i, carry):
            cols = pl.ds(pl.multiple_of(i * 128, 128), 128)
            wot[cols, :] = wo[:, cols].T
            return carry

        lax.fori_loop(0, width // 128, out_part, 0)

    def step(t, carry):
        @pl.when(t == jnp.where(is_last, 0, micro_count))
        def _():
            transpose_weights()

        m = jnp.where(is_last, t // 2, lax.rem(t, micro_count))
        back = jnp.where(is_last, lax.rem(t, 2), t // micro_count)

        @pl.when(back == 0)
        def _():
            forward(m)

        @pl.when(back == 1)
        def _():
            backward(m)

        return carry

    lax.fori_loop(0, 2 * micro_count, step, 0)

    @pl.when(is_odd)
    def _():
        for m in range(micro_count):
            output_back(m).start()

    @pl.when(section > 0)
    def _():
        start_core(3)

    farthest = x_count // 2

    def x_part(way, distance):
        if distance == farthest:
            return pl.ds(way * (dp_rows // 2), dp_rows // 2)
        return pl.ds(0, dp_rows)

    def x_target(way, distance):
        step = distance if way == 0 else -distance
        return lax.rem(x_id + step + x_count, x_count)

    def x_copy(c, way, distance):
        part = x_part(way, distance)
        return pltpu.make_async_remote_copy(
            src_ref=xs.at[c, x_target(way, distance), part, :],
            dst_ref=x_in.at[c, way, distance - 1, part, :],
            send_sem=ring_x_send.at[c, way, distance - 1],
            recv_sem=ring_x_recv.at[c, way, distance - 1],
            device_id=at_x(1 if way == 0 else -1),
            device_id_type=MESH,
        )

    def start_x(c):
        for x in range(x_count):
            core_copy(c, x).wait_recv()
            xs[c, x] = (
                cw[c, block_rows(x, core), :].astype(jnp.float32)
                + core_in[c, x].astype(jnp.float32)
            ).astype(jnp.bfloat16)
        for way in range(2):
            x_copy(c, way, farthest).start()

    def next_x(c, distance):
        for way in range(2):
            x_copy(c, way, distance + 1).wait_recv()
            target = x_target(way, distance)
            part = x_part(way, distance + 1)
            xs[c, target, part, :] = (
                xs[c, target, part, :].astype(jnp.float32)
                + x_in[c, way, distance, part, :].astype(jnp.float32)
            ).astype(jnp.bfloat16)
            x_copy(c, way, distance).start()

    def z_copy(c, step):
        target = lax.rem(seq_id + step, seq_count)
        return pltpu.make_async_remote_copy(
            src_ref=zs.at[c, target],
            dst_ref=z_in.at[c, seq_id],
            send_sem=z_send.at[c, step],
            recv_sem=z_recv.at[c, seq_id],
            device_id=at_z(step),
            device_id_type=MESH,
        )

    def start_z(c):
        total = xs[c, x_id].astype(jnp.float32)
        for way in range(2):
            x_copy(c, way, 1).wait_recv()
            total = total + x_in[c, way, 0].astype(jnp.float32)
        block_sum[...] = total
        for k in range(seq_count):
            zs[c, k] = block_sum[k * own_rows : (k + 1) * own_rows, :].astype(jnp.bfloat16)
        for step in range(1, seq_count):
            z_copy(c, step).start()

    def finish(c):
        total = zs[c, seq_id].astype(jnp.float32)
        for step in range(1, seq_count):
            source = lax.rem(seq_id + step, seq_count)
            landed = z_in.at[c, source]
            pltpu.make_async_copy(landed, landed, z_recv.at[c, source]).wait()
            total = total + z_in[c, source].astype(jnp.float32)
        if c < 3:
            grad_qkv_ref[:, 0, c * inner : (c + 1) * inner] = total
        else:
            grad_out_ref[:, 0, :] = total

    start_x(3)
    start_core(0)
    start_core(1)
    start_x(0)
    start_core(2)
    start_x(1)
    order = (3, 0, 1, 2)
    for distance in range(farthest - 1, 0, -1):
        for c in order:
            if c == 0 and distance == farthest - 1:
                start_x(2)
            next_x(c, distance)
    for c in order:
        start_z(c)
    for c in order:
        finish(c)

    for c in range(chunks):
        for x in range(x_count):
            core_copy(c, x).wait_send()
        for way in range(2):
            for d in range(1, farthest + 1):
                x_copy(c, way, d).wait_send()
        for step in range(1, seq_count):
            z_copy(c, step).wait_send()

    for m in range(micro_count):

        @pl.when(jnp.logical_and(section > 0, section < section_count - 1))
        def _():
            sent_forward(m, 0, seq_count)

        @pl.when(section > 0)
        def _():
            for k in range(seq_count):
                hop(bb, gb, g_send, g_recv, m, k, -1).wait_send()

        @pl.when(is_odd)
        def _():
            output_back(m).wait_send()
            output_own(m).wait()

        @pl.when(jnp.logical_not(is_odd))
        def _():
            pltpu.make_async_copy(out_hbm.at[m], out_hbm.at[m], o_recv.at[m]).wait()


def relay(seq_count, section_count, x, w_qkv, w_out, g):
    micro_count, rows, width = x.shape
    inner = w_out.shape[0]
    pairs = inner // (2 * HEAD_DIM)
    bf16, f32 = jnp.bfloat16, jnp.float32
    tokens = (micro_count, rows, width)
    dma = pltpu.SemaphoreType.DMA
    dp_count = lax.axis_size("dp")
    x_count = dp_count // 2
    dp_rows = width // dp_count
    own_rows = dp_rows // seq_count
    any_spec = pl.BlockSpec(memory_space=pl.ANY)
    vmem_spec = pl.BlockSpec(memory_space=pltpu.VMEM)
    return pl.pallas_call(
        functools.partial(relay_kernel, seq_count, section_count),
        out_shape=(
            jax.ShapeDtypeStruct(tokens, bf16),
            jax.ShapeDtypeStruct((own_rows, 1, 3 * inner), f32),
            jax.ShapeDtypeStruct((own_rows, 1, inner), f32),
        ),
        in_specs=[any_spec] * 4,
        out_specs=(any_spec, vmem_spec, vmem_spec),
        scratch_shapes=[
            pltpu.VMEM((width, 3 * inner), bf16),
            pltpu.VMEM((inner, width), bf16),
            pltpu.VMEM(tokens, bf16),
            pltpu.VMEM(tokens, bf16),
            pltpu.VMEM(tokens, f32),
            pltpu.VMEM((micro_count, rows, 128), f32),
            pltpu.VMEM(tokens, bf16),
            pltpu.VMEM((micro_count, rows, 3 * inner), bf16),
            pltpu.VMEM((micro_count, pairs, 2 * rows, rows), f32),
            pltpu.VMEM((micro_count, rows, inner), bf16),
            pltpu.VMEM((micro_count, rows, 3 * inner), bf16),
            pltpu.VMEM(tokens, bf16),
            pltpu.VMEM(tokens, bf16),
            dma((4,)),
            dma((micro_count, seq_count)),
            dma((micro_count, seq_count)),
            dma((micro_count, seq_count)),
            dma((micro_count, seq_count)),
            dma((micro_count,)),
            dma((micro_count,)),
            pltpu.VMEM((4, width, inner), bf16),
            pltpu.VMEM((4, x_count, dp_rows, inner), bf16),
            pltpu.VMEM((4, x_count, dp_rows, inner), bf16),
            pltpu.VMEM((4, 2, x_count // 2, dp_rows, inner), bf16),
            pltpu.VMEM((dp_rows, inner), f32),
            pltpu.VMEM((4, seq_count, own_rows, inner), bf16),
            pltpu.VMEM((4, seq_count, own_rows, inner), bf16),
            dma((4, x_count)),
            dma((4, x_count)),
            dma((4, 2, x_count // 2)),
            dma((4, 2, x_count // 2)),
            dma((4, seq_count)),
            dma((4, seq_count)),
            pltpu.SemaphoreType.REGULAR((2 * micro_count,)),
            pltpu.VMEM((3 * inner, width), bf16),
            pltpu.VMEM((width, inner), bf16),
        ],
        compiler_params=pltpu.CompilerParams(
            collective_id=0, has_side_effects=True, vmem_limit_bytes=60 * 1024 * 1024
        ),
        name="relay",
    )(x, w_qkv, w_out, g)


def local(clips_in, w_qkv, w_out, out_cotangent):
    seq_count = lax.axis_size("seq")
    section_count = lax.axis_size("section")
    micro_count, frames, patches_dev, width = clips_in.shape
    x = clips_in.reshape(micro_count, frames * patches_dev, width)
    g = out_cotangent.reshape(micro_count, -1, width)
    outputs, grad_qkv, grad_out = relay(seq_count, section_count, x, w_qkv[0], w_out[0], g)
    return (outputs.reshape((1,) + out_cotangent.shape), grad_qkv.transpose(1, 0, 2), grad_out.transpose(1, 0, 2))


def solution(mesh):
    return jax.shard_map(
        local,
        mesh=mesh,
        in_specs=(
            P("dp", None, "seq", None),
            P("section", None, None),
            P("section", None, None),
            P("dp", "seq", None, None),
        ),
        out_specs=(
            P("section", "dp", "seq", None, None),
            P("section", ("dp", "seq"), None),
            P("section", ("dp", "seq"), None),
        ),
        check_vma=False,
    )
```

```python
import functools
import math

import jax
import jax.numpy as jnp
from jax import lax
from jax.experimental import pallas as pl
from jax.experimental.pallas import tpu as pltpu
from jax.sharding import PartitionSpec as P

HEAD_DIM = 64
NORM_EPS = 1e-05
MASKED = -1e30
MESH = pl.DeviceIdType.MESH


def dot(a, b, a_dim, b_dim):
    return lax.dot_general(
        a, b, (((a_dim,), (b_dim,)), ((), ())), preferred_element_type=jnp.float32
    )


def relay_kernel(
    seq_count,
    section_count,
    x_hbm,
    w_qkv_hbm,
    w_out_hbm,
    g_hbm,
    out_hbm,
    grad_qkv_ref,
    grad_out_ref,
    wq,
    wo,
    xb,
    gb,
    ub,
    rb,
    nb,
    pk,
    pr,
    mx,
    dpk,
    hb,
    bb,
    in_sem,
    x_send,
    x_recv,
    g_send,
    g_recv,
    o_send,
    o_recv,
    cw,
    core_in,
    xs,
    x_in,
    block_sum,
    zs,
    z_in,
    core_send,
    core_recv,
    ring_x_send,
    ring_x_recv,
    z_send,
    z_recv,
    turn,
    wqt,
    wot,
):
    dp_id = lax.axis_index("dp")
    section = lax.axis_index("section")
    seq_id = lax.axis_index("seq")
    micro_count, rows, width = xb.shape
    block = rows // seq_count
    inner = wo.shape[0]
    pairs = inner // (2 * HEAD_DIM)
    scale = 1.0 / math.sqrt(HEAD_DIM)
    dp_count = lax.axis_size("dp")
    x_count = dp_count // 2
    x_id = dp_id // 2
    core = lax.rem(dp_id, 2)
    is_first = section == 0
    is_last = section == section_count - 1
    is_odd = lax.rem(section, 2) == 1

    load_wq = pltpu.make_async_copy(w_qkv_hbm, wq, in_sem.at[0])
    load_wo = pltpu.make_async_copy(w_out_hbm, wo, in_sem.at[1])
    load_x = pltpu.make_async_copy(x_hbm, xb, in_sem.at[2])
    load_g = pltpu.make_async_copy(g_hbm, gb, in_sem.at[3])

    @pl.when(is_first)
    def _():
        load_x.start()

    load_wq.start()
    load_wo.start()

    @pl.when(is_last)
    def _():
        load_g.start()

    barrier = pltpu.get_barrier_semaphore()

    @pl.when(section > 0)
    def _():
        for k in range(seq_count):
            pl.semaphore_signal(
                barrier, inc=1, device_id=(dp_id, section - 1, k), device_id_type=MESH
            )

    @pl.when(section < section_count - 1)
    def _():
        for k in range(seq_count):
            pl.semaphore_signal(
                barrier, inc=1, device_id=(dp_id, section + 1, k), device_id_type=MESH
            )

    def at_x(step):
        return (2 * lax.rem(x_id + step + x_count, x_count) + core, section, seq_id)

    def at_z(step):
        return (dp_id, section, lax.rem(seq_id + step + seq_count, seq_count))

    other_core = (2 * x_id + 1 - core, section, seq_id)
    peers = [other_core, at_x(1), at_x(-1)] + [at_z(step) for step in range(1, seq_count)]
    for peer in peers:
        pl.semaphore_signal(barrier, inc=1, device_id=peer, device_id_type=MESH)

    def wait_for_peers():
        inner_section = jnp.logical_and(section > 0, section < section_count - 1)
        hops = jnp.where(inner_section, 2 * seq_count, seq_count)
        pl.semaphore_wait(barrier, hops + len(peers))


    def hop(src, dst, send, recv, m, k, step):
        return pltpu.make_async_remote_copy(
            src_ref=src.at[m, pl.ds(k * block, block), :],
            dst_ref=dst.at[m, pl.ds(seq_id * block, block), :],
            send_sem=send.at[m, k],
            recv_sem=recv.at[m, seq_id],
            device_id=(dp_id, section + step, k),
            device_id_type=MESH,
        )

    def arrival(dst, recv, m, k):
        landed = dst.at[m, pl.ds(k * block, block), :]
        return pltpu.make_async_copy(landed, landed, recv.at[m, k])

    def output_back(m):
        return pltpu.make_async_remote_copy(
            src_ref=xb.at[m],
            dst_ref=out_hbm.at[m],
            send_sem=o_send.at[m],
            recv_sem=o_recv.at[m],
            device_id=(dp_id, section - 1, seq_id),
            device_id_type=MESH,
        )

    def output_own(m):
        return pltpu.make_async_copy(hb.at[m], out_hbm.at[m], o_recv.at[m])

    lane = lax.broadcasted_iota(jnp.int32, (rows, 2 * HEAD_DIM), 1)
    first_head = lane < HEAD_DIM
    row_group = lax.rem(lax.broadcasted_iota(jnp.int32, (2 * rows, rows), 0), block)
    col_group = lax.rem(lax.broadcasted_iota(jnp.int32, (2 * rows, rows), 1), block)
    same_group = jnp.where(row_group == col_group, 1, 0) + jnp.where(is_odd, 1, 0) > 0

    def stacked(part):
        zero = jnp.zeros_like(part)
        return jnp.concatenate(
            [jnp.where(first_head, part, zero), jnp.where(first_head, zero, part)], axis=0
        )

    def joined(part):
        return jnp.where(first_head, part[:rows], part[rows:])

    tile = 256 if width % 256 == 0 else 128
    tokens = micro_count * rows
    dp_rows = width // dp_count
    own_rows = dp_rows // seq_count
    chunks = 4

    def partial_grads(c):
        if c < 3:
            right = dpk[:, :, c * inner : (c + 1) * inner].reshape(tokens, inner)
            left_ref = nb
        else:
            right = mx[...].reshape(tokens, inner)
            left_ref = gb

        def rows_of(i, carry):
            cols = pl.ds(pl.multiple_of(i * tile, tile), tile)
            left = left_ref[:, :, cols].reshape(tokens, tile)
            cw[c, cols, :] = dot(left, right, 0, 0).astype(jnp.bfloat16)
            return carry

        lax.fori_loop(0, width // tile, rows_of, 0)

    def block_rows(x, of_core):
        return pl.ds(pl.multiple_of((2 * x + of_core) * dp_rows, dp_rows), dp_rows)

    def core_copy(c, x):
        return pltpu.make_async_remote_copy(
            src_ref=cw.at[c, block_rows(x, 1 - core), :],
            dst_ref=core_in.at[c, x],
            send_sem=core_send.at[c, x],
            recv_sem=core_recv.at[c, x],
            device_id=other_core,
            device_id_type=MESH,
        )

    def start_core(c):
        partial_grads(c)
        for x in range(x_count):
            core_copy(c, x).start()

    def start_forward(m):
        for k in range(seq_count):
            hop(hb, xb, x_send, x_recv, m, k, 1).start()

    def sent_forward(m, first, last):
        for k in range(first, last):
            hop(hb, xb, x_send, x_recv, m, k, 1).wait_send()

    def send_in_turns():
        early = (3 * seq_count) // 4
        for m in range(micro_count):
            for c in range(2):
                turn_id = 2 * m + c

                @pl.when(core == c)
                def _():
                    if turn_id > 0:
                        pl.semaphore_wait(turn.at[turn_id - 1], 1)
                        start_forward(m)
                    sent_forward(m, 0, early)
                    if turn_id < 2 * micro_count - 1:
                        pl.semaphore_signal(
                            turn.at[turn_id], inc=1, device_id=other_core, device_id_type=MESH
                        )
                    sent_forward(m, early, seq_count)

    def forward(m):
        @pl.when(section > 0)
        def _():
            for k in range(seq_count):
                arrival(xb, x_recv, m, k).wait()

        values = xb[m].astype(jnp.float32)
        centred = values - jnp.mean(values, axis=-1, keepdims=True)
        inverse = lax.rsqrt(jnp.mean(centred * centred, axis=-1, keepdims=True) + NORM_EPS)
        unit = centred * inverse
        ub[m] = unit
        rb[m] = jnp.broadcast_to(inverse, (rows, 128))
        nb[m] = unit.astype(jnp.bfloat16)
        pk[m] = dot(nb[m], wq[...], 1, 0).astype(jnp.bfloat16)
        for p in range(pairs):
            cols = pl.ds(p * 128, 128)
            query = pk[m, :, pl.ds(p * 128, 128)]
            key = pk[m, :, pl.ds(inner + p * 128, 128)]
            value = pk[m, :, pl.ds(2 * inner + p * 128, 128)]
            scores = dot(stacked(query), key, 1, 1) * scale
            scores = jnp.where(same_group, scores, MASKED)
            exps = jnp.exp(scores - jnp.max(scores, axis=-1, keepdims=True))
            probs = exps * (1.0 / jnp.sum(exps, axis=-1, keepdims=True))
            pr[m, p] = probs
            mx[m, :, cols] = joined(dot(probs.astype(jnp.bfloat16), value, 1, 0)).astype(
                jnp.bfloat16
            )
        hb[m] = (xb[m].astype(jnp.float32) + dot(mx[m], wo[...], 1, 0)).astype(jnp.bfloat16)

        @pl.when(m == 0)
        def _():
            wait_for_peers()

        @pl.when(jnp.logical_and(section > 0, section < section_count - 1))
        def _():
            start_forward(m)

        @pl.when(jnp.logical_and(is_first, core + m == 0))
        def _():
            start_forward(0)

        @pl.when(jnp.logical_and(is_first, m == micro_count - 1))
        def _():
            send_in_turns()

        @pl.when(is_odd)
        def _():
            output_own(m).start()

    def backward(m):
        @pl.when(section < section_count - 1)
        def _():
            for k in range(seq_count):
                arrival(gb, g_recv, m, k).wait()

        @pl.when(jnp.logical_and(is_first, m == micro_count - 1))
        def _():
            start_core(3)

        d_mixed = dot(gb[m], wot[...], 1, 0).astype(jnp.bfloat16)
        for p in range(pairs):
            query = stacked(pk[m, :, pl.ds(p * 128, 128)])
            key = pk[m, :, pl.ds(inner + p * 128, 128)]
            value = pk[m, :, pl.ds(2 * inner + p * 128, 128)]
            d_heads = stacked(d_mixed[:, p * 128 : (p + 1) * 128])
            probs = pr[m, p]
            d_values = dot(probs.astype(jnp.bfloat16), d_heads, 0, 0)
            d_probs = dot(d_heads, value, 1, 1)
            d_scores = probs * (d_probs - jnp.sum(probs * d_probs, axis=-1, keepdims=True))
            d_scores = d_scores.astype(jnp.bfloat16)
            d_query = joined(dot(d_scores, key, 1, 0)) * scale
            d_keys = dot(d_scores, query, 0, 0) * scale
            dpk[m, :, pl.ds(p * 128, 128)] = d_query.astype(jnp.bfloat16)
            dpk[m, :, pl.ds(inner + p * 128, 128)] = d_keys.astype(jnp.bfloat16)
            dpk[m, :, pl.ds(2 * inner + p * 128, 128)] = d_values.astype(jnp.bfloat16)

        @pl.when(section > 0)
        def _():
            d_normed = dot(dpk[m], wqt[...], 1, 0)
            unit = ub[m]
            d_inside = rb[m, :, 0:1] * (
                d_normed
                - jnp.mean(d_normed, axis=-1, keepdims=True)
                - unit * jnp.mean(d_normed * unit, axis=-1, keepdims=True)
            )
            bb[m] = (gb[m].astype(jnp.float32) + d_inside).astype(jnp.bfloat16)
            for k in range(seq_count):
                hop(bb, gb, g_send, g_recv, m, k, -1).start()

    @pl.when(is_first)
    def _():
        load_x.wait()

    load_wq.wait()
    load_wo.wait()

    @pl.when(is_last)
    def _():
        load_g.wait()

    def transpose_weights():
        def part(i, carry):
            cols = pl.ds(pl.multiple_of(i * 128, 128), 128)
            wqt[cols, :] = wq[:, cols].T
            return carry

        @pl.when(section > 0)
        def _():
            lax.fori_loop(0, 3 * inner // 128, part, 0)

        def out_part(i, carry):
            cols = pl.ds(pl.multiple_of(i * 128, 128), 128)
            wot[cols, :] = wo[:, cols].T
            return carry

        lax.fori_loop(0, width // 128, out_part, 0)

    def step(t, carry):
        @pl.when(t == jnp.where(is_last, 0, micro_count))
        def _():
            transpose_weights()

        m = jnp.where(is_last, t // 2, lax.rem(t, micro_count))
        back = jnp.where(is_last, lax.rem(t, 2), t // micro_count)

        @pl.when(back == 0)
        def _():
            forward(m)

        @pl.when(back == 1)
        def _():
            backward(m)

        return carry

    lax.fori_loop(0, 2 * micro_count, step, 0)

    @pl.when(is_odd)
    def _():
        for m in range(micro_count):
            output_back(m).start()

    @pl.when(section > 0)
    def _():
        start_core(3)

    farthest = x_count // 2

    def x_part(way, distance):
        if distance == farthest:
            return pl.ds(way * (dp_rows // 2), dp_rows // 2)
        return pl.ds(0, dp_rows)

    def x_target(way, distance):
        step = distance if way == 0 else -distance
        return lax.rem(x_id + step + x_count, x_count)

    def x_copy(c, way, distance):
        part = x_part(way, distance)
        return pltpu.make_async_remote_copy(
            src_ref=xs.at[c, x_target(way, distance), part, :],
            dst_ref=x_in.at[c, way, distance - 1, part, :],
            send_sem=ring_x_send.at[c, way, distance - 1],
            recv_sem=ring_x_recv.at[c, way, distance - 1],
            device_id=at_x(1 if way == 0 else -1),
            device_id_type=MESH,
        )

    def start_x(c):
        for x in range(x_count):
            core_copy(c, x).wait_recv()
            xs[c, x] = (
                cw[c, block_rows(x, core), :].astype(jnp.float32)
                + core_in[c, x].astype(jnp.float32)
            ).astype(jnp.bfloat16)
        for way in range(2):
            x_copy(c, way, farthest).start()

    def next_x(c, distance):
        for way in range(2):
            x_copy(c, way, distance + 1).wait_recv()
            target = x_target(way, distance)
            part = x_part(way, distance + 1)
            xs[c, target, part, :] = (
                xs[c, target, part, :].astype(jnp.float32)
                + x_in[c, way, distance, part, :].astype(jnp.float32)
            ).astype(jnp.bfloat16)
            x_copy(c, way, distance).start()

    def z_copy(c, step):
        target = lax.rem(seq_id + step, seq_count)
        return pltpu.make_async_remote_copy(
            src_ref=zs.at[c, target],
            dst_ref=z_in.at[c, seq_id],
            send_sem=z_send.at[c, step],
            recv_sem=z_recv.at[c, seq_id],
            device_id=at_z(step),
            device_id_type=MESH,
        )

    def start_z(c):
        total = xs[c, x_id].astype(jnp.float32)
        for way in range(2):
            x_copy(c, way, 1).wait_recv()
            total = total + x_in[c, way, 0].astype(jnp.float32)
        block_sum[...] = total
        for k in range(seq_count):
            zs[c, k] = block_sum[k * own_rows : (k + 1) * own_rows, :].astype(jnp.bfloat16)
        for step in range(1, seq_count):
            z_copy(c, step).start()

    def finish(c):
        total = zs[c, seq_id].astype(jnp.float32)
        for step in range(1, seq_count):
            source = lax.rem(seq_id + step, seq_count)
            landed = z_in.at[c, source]
            pltpu.make_async_copy(landed, landed, z_recv.at[c, source]).wait()
            total = total + z_in[c, source].astype(jnp.float32)
        if c < 3:
            grad_qkv_ref[:, 0, c * inner : (c + 1) * inner] = total
        else:
            grad_out_ref[:, 0, :] = total

    start_x(3)
    start_core(0)
    start_core(1)
    start_x(0)
    start_core(2)
    start_x(1)
    order = (3, 0, 1, 2)
    for distance in range(farthest - 1, 0, -1):
        for c in order:
            if c == 0 and distance == farthest - 1:
                start_x(2)
            next_x(c, distance)
    for c in order:
        start_z(c)
    for c in order:
        finish(c)

    for c in range(chunks):
        for x in range(x_count):
            core_copy(c, x).wait_send()
        for way in range(2):
            for d in range(1, farthest + 1):
                x_copy(c, way, d).wait_send()
        for step in range(1, seq_count):
            z_copy(c, step).wait_send()

    for m in range(micro_count):

        @pl.when(jnp.logical_and(section > 0, section < section_count - 1))
        def _():
            sent_forward(m, 0, seq_count)

        @pl.when(section > 0)
        def _():
            for k in range(seq_count):
                hop(bb, gb, g_send, g_recv, m, k, -1).wait_send()

        @pl.when(is_odd)
        def _():
            output_back(m).wait_send()
            output_own(m).wait()

        @pl.when(jnp.logical_not(is_odd))
        def _():
            pltpu.make_async_copy(out_hbm.at[m], out_hbm.at[m], o_recv.at[m]).wait()


def relay(seq_count, section_count, x, w_qkv, w_out, g):
    micro_count, rows, width = x.shape
    inner = w_out.shape[0]
    pairs = inner // (2 * HEAD_DIM)
    bf16, f32 = jnp.bfloat16, jnp.float32
    tokens = (micro_count, rows, width)
    dma = pltpu.SemaphoreType.DMA
    dp_count = lax.axis_size("dp")
    x_count = dp_count // 2
    dp_rows = width // dp_count
    own_rows = dp_rows // seq_count
    any_spec = pl.BlockSpec(memory_space=pl.ANY)
    vmem_spec = pl.BlockSpec(memory_space=pltpu.VMEM)
    return pl.pallas_call(
        functools.partial(relay_kernel, seq_count, section_count),
        out_shape=(
            jax.ShapeDtypeStruct(tokens, bf16),
            jax.ShapeDtypeStruct((own_rows, 1, 3 * inner), f32),
            jax.ShapeDtypeStruct((own_rows, 1, inner), f32),
        ),
        in_specs=[any_spec] * 4,
        out_specs=(any_spec, vmem_spec, vmem_spec),
        scratch_shapes=[
            pltpu.VMEM((width, 3 * inner), bf16),
            pltpu.VMEM((inner, width), bf16),
            pltpu.VMEM(tokens, bf16),
            pltpu.VMEM(tokens, bf16),
            pltpu.VMEM(tokens, f32),
            pltpu.VMEM((micro_count, rows, 128), f32),
            pltpu.VMEM(tokens, bf16),
            pltpu.VMEM((micro_count, rows, 3 * inner), bf16),
            pltpu.VMEM((micro_count, pairs, 2 * rows, rows), f32),
            pltpu.VMEM((micro_count, rows, inner), bf16),
            pltpu.VMEM((micro_count, rows, 3 * inner), bf16),
            pltpu.VMEM(tokens, bf16),
            pltpu.VMEM(tokens, bf16),
            dma((4,)),
            dma((micro_count, seq_count)),
            dma((micro_count, seq_count)),
            dma((micro_count, seq_count)),
            dma((micro_count, seq_count)),
            dma((micro_count,)),
            dma((micro_count,)),
            pltpu.VMEM((4, width, inner), bf16),
            pltpu.VMEM((4, x_count, dp_rows, inner), bf16),
            pltpu.VMEM((4, x_count, dp_rows, inner), bf16),
            pltpu.VMEM((4, 2, x_count // 2, dp_rows, inner), bf16),
            pltpu.VMEM((dp_rows, inner), f32),
            pltpu.VMEM((4, seq_count, own_rows, inner), bf16),
            pltpu.VMEM((4, seq_count, own_rows, inner), bf16),
            dma((4, x_count)),
            dma((4, x_count)),
            dma((4, 2, x_count // 2)),
            dma((4, 2, x_count // 2)),
            dma((4, seq_count)),
            dma((4, seq_count)),
            pltpu.SemaphoreType.REGULAR((2 * micro_count,)),
            pltpu.VMEM((3 * inner, width), bf16),
            pltpu.VMEM((width, inner), bf16),
        ],
        compiler_params=pltpu.CompilerParams(
            collective_id=0, has_side_effects=True, vmem_limit_bytes=60 * 1024 * 1024
        ),
        name="relay",
    )(x, w_qkv, w_out, g)


def hand_over_kernel(*refs):
    count = (len(refs) - 2) // 3
    sources, results, buffers = refs[:count], refs[count : 2 * count], refs[2 * count : 3 * count]
    in_sem, out_sem = refs[3 * count :]
    loads = [pltpu.make_async_copy(sources[i], buffers[i], in_sem.at[i]) for i in range(count)]
    stores = [pltpu.make_async_copy(buffers[i], results[i], out_sem.at[i]) for i in range(count)]
    for load in loads:
        load.start()
    for load, store in zip(loads, stores):
        load.wait()
        store.start()
    for store in stores:
        store.wait()


def hand_over(*arrays):
    count = len(arrays)
    any_spec = pl.BlockSpec(memory_space=pl.ANY)
    return pl.pallas_call(
        hand_over_kernel,
        out_shape=tuple(jax.ShapeDtypeStruct(a.shape, a.dtype) for a in arrays),
        in_specs=[any_spec] * count,
        out_specs=(any_spec,) * count,
        scratch_shapes=[pltpu.VMEM(a.shape, a.dtype) for a in arrays]
        + [pltpu.SemaphoreType.DMA((count,)), pltpu.SemaphoreType.DMA((count,))],
        name="hand_over",
    )(*arrays)


def local(clips_in, w_qkv, w_out, out_cotangent):
    seq_count = lax.axis_size("seq")
    section_count = lax.axis_size("section")
    micro_count, frames, patches_dev, width = clips_in.shape
    x = clips_in.reshape(micro_count, frames * patches_dev, width)
    g = out_cotangent.reshape(micro_count, -1, width)
    outputs, grad_qkv, grad_out = hand_over(
        *relay(seq_count, section_count, x, w_qkv[0], w_out[0], g)
    )
    return (outputs.reshape((1,) + out_cotangent.shape), grad_qkv.transpose(1, 0, 2), grad_out.transpose(1, 0, 2))


def solution(mesh):
    return jax.shard_map(
        local,
        mesh=mesh,
        in_specs=(
            P("dp", None, "seq", None),
            P("section", None, None),
            P("section", None, None),
            P("dp", "seq", None, None),
        ),
        out_specs=(
            P("section", "dp", "seq", None, None),
            P("section", ("dp", "seq"), None),
            P("section", ("dp", "seq"), None),
        ),
        check_vma=False,
    )
```
